32 devices in a mesh: ent: 8 (over z, y), rep: 4 (over x, core).
Axes of the slice: x: 2, y: 2, z: 4, core: 2. Of those that a mesh axis runs over, the one named last changes fastest.
Arguments:
- facts: bfloat16 [65536, 512], P(('ent', 'rep')), may hold values from -6 to 6
- fact_owner: int32 [65536, 1], P(('ent', 'rep')), may hold values from 0 to 7; in each aligned block of 2048 rows (0 to 2047, 2048 to 4095, ...) at most 512 rows name the same one
- fact_slot: int32 [65536], P(('ent', 'rep')), may hold values from 0 to 127
- entity_feats: bfloat16 [1024, 512], P('ent'), may hold values from -6 to 6
- out_cotangent: bfloat16 [1024, 512], P('ent'), may hold values from -6 to 6
- w_msg: bfloat16 [512, 512], replicated, may hold values from -0.25 to 0.25
- w_upd: bfloat16 [512, 512], replicated, may hold values from -0.25 to 0.25
Outputs:
- ent_out: bfloat16 [1024, 512], P('ent')
- fact_grad: bfloat16 [65536, 512], P(('ent', 'rep'))
- msg_weight_grad: float32 [512, 512], P(('ent', 'rep'))
- upd_weight_grad_t: float32 [512, 512], P(('ent', 'rep'))
The draws below stay inside these ranges and needn't reach their ends.
Inputs may be any that keep to these rules, and one draw needn't show every extreme that they name: `fact_owner`: among the rows of one device, at most 512 name the same owner.
All inputs are finite; a program needn't handle non-finite values.
Results may differ from the reference program's by a relative error of at most 0.0065.
Values may be sent and summed in bfloat16 or wider, within the bound.
A program may use at most 64 MiB of HBM per device.

```python
import math
import jax
import jax.numpy as jnp
import numpy as np
from jax import lax

D = 512
F_DEV = 2048
ENT_DEV = 128
CAP = 512
FACTS = 65536
ENTS = 1024
N_ENT = 8


def with_ends(entries, key, smallest, high):
    spot = [jax.random.randint(jax.random.fold_in(key, axis), (), 0, length) for axis, length in enumerate(entries.shape)]
    longest = entries.shape.index(max(entries.shape))
    neighbour = spot[:longest] + [(spot[longest] + 1) % entries.shape[longest]] + spot[longest + 1:]
    return entries.at[tuple(spot)].set(smallest).at[tuple(neighbour)].set(high)


def spiked(entries, own_key, source, target, parts, factor):
    owner, partner = [(jnp.arange(entries.shape[axis_at]) // (entries.shape[axis_at] // parts)).reshape([-1 if axis == axis_at else 1 for axis in range(entries.ndim)]) for axis_at in (source, target)]
    chosen = jax.random.permutation(own_key, parts)[partner]
    strong = (owner == chosen) | (owner == (partner + parts // 2) % parts)
    return jnp.where(strong, factor * entries, entries)


def level_of(stream_key, extent, cuts, smallest, largest):
    def one(position, shards_of):
        steps = jax.random.uniform(jax.random.fold_in(jax.random.fold_in(stream_key, 6), position), (shards_of,), jnp.float32, smallest / len(cuts), largest / len(cuts))
        return jnp.repeat(jnp.exp(steps), extent[position] // shards_of).reshape((-1,) + (1,) * (len(extent) - position - 1))

    loudness = one(*cuts[0])
    for cut in cuts[1:]:
        loudness = loudness * one(*cut)
    return loudness


def rank_bounds(amount, slope):
    portions = [(1 << 20) // math.isqrt(standing ** slope) + 1 for standing in range(1, amount + 1)]
    deviation = 1 + sum(portions) // (1 << 30)
    return np.cumsum(np.array([max(1, weight // deviation) for weight in portions]))


def skewed_ids(stream_key, dims, number_of, slope):
    listing = rank_bounds(number_of, slope)
    pick = jax.random.randint(jax.random.fold_in(stream_key, 1), dims, 0, int(listing[number_of - 1]))
    grade = jnp.searchsorted(jnp.asarray(listing, jnp.int32), pick, side="right")
    return jax.random.permutation(jax.random.fold_in(stream_key, 2), number_of)[grade].astype(jnp.int32)


def deal_out(rng, own, number, rows, amount, top, most, skew):
    order = jax.random.permutation(rng, amount)
    crowded, ordinary = portions_of(amount, rows * top, most, skew, True), portions_of(amount, rows * top, most, skew, False)
    places = jnp.arange(amount)

    def named(sizes, turn):
        used = int((sizes > 0).sum())
        fixed = max(1, used // 4)
        moved = fixed + (places - fixed + turn * (used - fixed)) % max(1, amount - fixed)
        return jnp.zeros((amount,), jnp.int32).at[order[jnp.where(places < fixed, places, moved)]].set(jnp.asarray(sizes, jnp.int32))

    sizes = jnp.where(number % 4 == 0, named(crowded, number // 4), named(ordinary, number - number // 4 - 1))
    mixed = jax.random.permutation(jax.random.fold_in(own, 3), amount)
    source_of, sink = mixed[0:amount // 2 * 2:2], mixed[1:amount // 2 * 2:2]
    slack = jnp.minimum(sizes[source_of] - 1, most - sizes[sink]) // 2
    slack = jnp.where((source_of == order[0]) | (sink == order[0]) | (sizes[sink] == 0), 0, jnp.maximum(slack, 0))
    moved = jax.random.randint(jax.random.fold_in(own, 4), (amount // 2,), 0, 1 << 20) % (slack + 1)
    sizes = sizes.at[source_of].add(-moved).at[sink].add(moved)
    items = jnp.searchsorted(jnp.cumsum(sizes), jnp.arange(rows * top), side="right").astype(jnp.int32)
    grid = items.reshape(top, rows).T
    grid = grid[jax.random.permutation(jax.random.fold_in(own, 1), rows)]
    turn = jax.random.randint(jax.random.fold_in(own, 2), (rows, 1), 0, top)
    return jnp.take_along_axis(grid, (jnp.arange(top)[None, :] + turn) % top, axis=1)


def portions_of(number_of, total, most, lean, full):
    loads = [(1 << 20) // math.isqrt(rank ** lean) + 1 for rank in range(1, number_of + 1)]
    largest = most if full else min(most, max(-(-total // number_of), total * loads[0] // sum(loads)))
    least = 1 if total - largest >= number_of - 1 else 0
    counts, surplus = [largest] + [least] * (number_of - 1), total - largest - least * (number_of - 1)
    while surplus > 0:
        free = [i for i in range(1, number_of) if counts[i] < largest] or [i for i in range(1, number_of) if counts[i] < most]
        whole, left = sum([loads[i] for i in free]), surplus
        for i in free:
            extra = min(most - counts[i], max(1, left * loads[i] // whole), surplus)
            counts[i] = counts[i] + extra
            surplus = surplus - extra
    return np.array(counts)


def bell_draw(stream_key, shape, spread, bound, split=(), dtype=jnp.bfloat16):
    loudness = level_of(stream_key, shape, split, -0.22, 0.18) if split else 1.0
    values = jax.random.normal(stream_key, shape, jnp.float32) * spread * loudness
    return jnp.minimum(jnp.maximum(values, -bound), bound).astype(dtype)


def heavy_noise(key, extent, deviation, most, cuts, heavy, kind=jnp.bfloat16):
    array = deviation * jax.random.normal(key, extent, jnp.float32)
    if cuts:
        array = array * level_of(key, extent, cuts, -0.22, 0.18)
    return jnp.clip(spiked(array, jax.random.fold_in(key, 3), *heavy), -most, most).astype(kind)


def setup_inputs(seed: int = 0) -> dict:
    key_of = jax.random.split(jax.random.key(seed), 8)
    facts = heavy_noise(key_of[0], (FACTS, D), 1.0, 6.0, ((0, 32),), (0, 1, 32, 2.75))
    fact_owner_keys = jax.random.split(jax.random.fold_in(key_of[1], 1), FACTS // F_DEV)
    fact_owner_turns = jax.random.permutation(jax.random.fold_in(key_of[1], 3), FACTS // F_DEV)
    fact_owner = jax.vmap(lambda own, number: deal_out(jax.random.fold_in(key_of[1], 2), own, number, F_DEV, N_ENT, 1, CAP, 2))(fact_owner_keys, fact_owner_turns).reshape((FACTS, 1))
    fact_slot = with_ends(skewed_ids(key_of[2], (FACTS,), ENT_DEV, 2), jax.random.fold_in(key_of[2], 3), 0, ENT_DEV - 1).astype(jnp.int32)
    entity_feats = bell_draw(key_of[3], (ENTS, D), 1.0, 6.0, ((0, 8),))
    out_cotangent = heavy_noise(key_of[4], (ENTS, D), 1.0, 6.0, ((0, 8),), (0, 1, 8, 2.0))
    w_msg = bell_draw(key_of[5], (D, D), D ** -0.5, 0.25)
    w_upd = bell_draw(key_of[6], (D, D), D ** -0.5, 0.25)
    return {"facts": facts, "fact_owner": fact_owner, "fact_slot": fact_slot, "entity_feats": entity_feats, "out_cotangent": out_cotangent, "w_msg": w_msg, "w_upd": w_upd}


def silu_grad(value):
    sig = jax.nn.sigmoid(value)
    return sig * (1.0 + value * (1.0 - sig))

def reference(facts, fact_owner, fact_slot, entity_feats, out_cotangent, w_msg, w_upd):
    key = (fact_owner[:, 0] * ENT_DEV + fact_slot).astype(jnp.int32)
    pre = jnp.dot(facts, w_msg, preferred_element_type=jnp.float32)
    message = jax.nn.silu(pre).astype(jnp.bfloat16)
    total = ENT_DEV * N_ENT
    agg = jax.ops.segment_sum(message.astype(jnp.float32), key, num_segments=total)
    count = jax.ops.segment_sum(jnp.ones(key.shape, jnp.float32), key, num_segments=total)
    denom = jnp.maximum(count, 1.0)[:, None]
    mean = (agg / denom).astype(jnp.bfloat16)
    zval = jnp.dot(mean, w_upd, preferred_element_type=jnp.float32)
    ent_out = (entity_feats.astype(jnp.float32) + jax.nn.silu(zval)).astype(jnp.bfloat16)
    grad_z = (out_cotangent.astype(jnp.float32) * silu_grad(zval)).astype(jnp.bfloat16)
    upd_t = lax.dot_general(grad_z, mean, (((0,), (0,)), ((), ())), preferred_element_type=jnp.float32)
    d_mean = lax.dot_general(grad_z, w_upd, (((1,), (1,)), ((), ())), preferred_element_type=jnp.float32)
    d_agg = (d_mean / denom).astype(jnp.bfloat16)
    d_msg = jnp.take(d_agg, key, axis=0)
    d_pre = (d_msg.astype(jnp.float32) * silu_grad(pre)).astype(jnp.bfloat16)
    msg_grad = lax.dot_general(facts, d_pre, (((0,), (0,)), ((), ())), preferred_element_type=jnp.float32)
    fact_grad = lax.dot_general(d_pre, w_msg, (((1,), (1,)), ((), ())), preferred_element_type=jnp.float32).astype(jnp.bfloat16)
    return (ent_out, fact_grad, msg_grad, upd_t)
```

```python
import functools

import jax
import jax.numpy as jnp
from jax import lax
from jax.experimental import pallas as pl
from jax.experimental.pallas import tpu as pltpu
from jax.sharding import PartitionSpec as P

E_HI, E_LO, R_HI, R_LO = range(4)
ALL = (E_HI, E_LO, R_HI, R_LO)
ORDER_A = (R_LO, R_HI, E_LO, E_HI)
ORDER_B = (R_LO, E_LO, R_HI, E_HI)
MESH = pl.DeviceIdType.MESH
VMEM_LIMIT = 60 << 20
CHUNKS = 2


def silu_grad(value):
    sig = jax.nn.sigmoid(value)
    return sig * (1.0 + value * (1.0 - sig))


def position():
    ent, rep = lax.axis_index("ent"), lax.axis_index("rep")
    return (ent // 2, lax.rem(ent, 2), rep // 2, lax.rem(rep, 2))


def device_at(here, dim, coord):
    if dim == E_HI:
        return {"ent": coord * 2 + here[E_LO]}
    if dim == E_LO:
        return {"ent": here[E_HI] * 2 + coord}
    if dim == R_HI:
        return {"rep": coord * 2 + here[R_LO]}
    return {"rep": here[R_HI] * 2 + coord}


def greet(grid, here):
    barrier = pltpu.get_barrier_semaphore()
    total = 0
    for dim in ALL:
        for step in range(1, grid[dim]):
            target = device_at(here, dim, lax.rem(here[dim] + step, grid[dim]))
            pl.semaphore_signal(barrier, inc=1, device_id=target, device_id_type=MESH)
            total += 1
    return total


def sum_scratch(grid, order, tail, dtype):
    left, shapes = [0, 1, 2, 3], []
    for dim in order:
        left.remove(dim)
        kept = tuple(grid[d] for d in left) + tail
        shapes += [
            pltpu.VMEM((grid[dim] - 1,) + kept, dtype),
            pltpu.VMEM(kept, jnp.float32),
            pltpu.VMEM(kept if left else (16, 128), dtype),
            pltpu.SemaphoreType.DMA((grid[dim] - 1,)),
            pltpu.SemaphoreType.DMA((grid[dim] - 1,)),
        ]
    return shapes


class Scatter:
    def __init__(self, grid, here, order, own, sent, scratch):
        self.grid, self.here, self.order, self.own, self.sent = grid, here, order, own, sent
        self.scratch, self.left, self.stage = scratch, [0, 1, 2, 3], 0

    def start(self):
        dim = self.order[self.stage]
        size, mine = self.grid[dim], self.here[dim]
        arrived, _, _, send, recv = self.scratch[5 * self.stage:5 * self.stage + 5]
        lead = (slice(None),) * self.left.index(dim)
        self.copies = []
        for step in range(1, size):
            coord = lax.rem(mine + step, size)
            copy = pltpu.make_async_remote_copy(
                src_ref=self.sent.at[lead + (coord,)],
                dst_ref=arrived.at[step - 1],
                send_sem=send.at[step - 1],
                recv_sem=recv.at[step - 1],
                device_id=device_at(self.here, dim, coord),
                device_id_type=MESH,
            )
            copy.start()
            self.copies.append(copy)

    def finish(self):
        dim = self.order[self.stage]
        arrived, total, rounded, _, _ = self.scratch[5 * self.stage:5 * self.stage + 5]
        lead = (slice(None),) * self.left.index(dim)
        value = self.own[lead + (self.here[dim],)]
        for index, copy in enumerate(self.copies):
            copy.wait()
            value = value + arrived[index].astype(jnp.float32)
        total[...] = value
        self.own = self.sent = total
        self.left.remove(dim)
        self.stage += 1
        if self.left and rounded.dtype != jnp.float32:
            rounded[...] = value.astype(rounded.dtype)
            self.sent = rounded

    def advance(self):
        self.finish()
        if self.stage < 4:
            self.start()


class Counts:
    def __init__(self, grid, here, order, table, scratch):
        self.grid, self.here, self.order, self.table = grid, here, order, table
        self.scratch, self.stage = scratch, 0

    def start(self):
        dim = self.order[self.stage]
        size, mine = self.grid[dim], self.here[dim]
        arrived, _, send, recv = self.scratch[4 * self.stage:4 * self.stage + 4]
        self.copies = []
        for step in range(1, size):
            copy = pltpu.make_async_remote_copy(
                src_ref=self.table,
                dst_ref=arrived.at[step - 1],
                send_sem=send.at[step - 1],
                recv_sem=recv.at[step - 1],
                device_id=device_at(self.here, dim, lax.rem(mine + step, size)),
                device_id_type=MESH,
            )
            copy.start()
            self.copies.append(copy)

    def advance(self):
        arrived, total, _, _ = self.scratch[4 * self.stage:4 * self.stage + 4]
        value = self.table[...]
        for index, copy in enumerate(self.copies):
            copy.wait()
            value = value + arrived[index]
        total[...] = value
        self.table = total
        self.stage += 1
        if self.stage < 4:
            self.start()


def count_scratch(grid, order, tail):
    shapes = []
    for dim in order:
        shapes += [
            pltpu.VMEM((grid[dim] - 1,) + tail, jnp.float32),
            pltpu.VMEM(tail, jnp.float32),
            pltpu.SemaphoreType.DMA((grid[dim] - 1,)),
            pltpu.SemaphoreType.DMA((grid[dim] - 1,)),
        ]
    return shapes


class Gather:
    def __init__(self, grid, here, dims, order, ref, sems):
        self.grid, self.here, self.dims, self.order = grid, here, dims, order
        self.ref, self.sems = ref, sems
        self.done, self.stage = [], 0

    def start(self):
        dim = self.order[self.stage]
        size, mine = self.grid[dim], self.here[dim]
        send, recv = self.sems[2 * self.stage:2 * self.stage + 2]
        index = tuple(slice(None) if d in self.done else self.here[d] for d in self.dims)
        block = self.ref.at[index]
        self.copies = []
        for step in range(1, size):
            coord = lax.rem(mine + step, size)
            copy = pltpu.make_async_remote_copy(
                src_ref=block,
                dst_ref=block,
                send_sem=send.at[step - 1],
                recv_sem=recv.at[step - 1],
                device_id=device_at(self.here, dim, coord),
                device_id_type=MESH,
            )
            copy.start()
            self.copies.append(copy)

    def advance(self):
        for copy in self.copies:
            copy.wait()
        self.done.append(self.order[self.stage])
        self.stage += 1
        if self.stage < len(self.order):
            self.start()


def gather_scratch(grid, order):
    return [pltpu.SemaphoreType.DMA((grid[d] - 1,)) for d in order for _ in range(2)]


def layer_kernel(grid, kept, facts_hbm, owner_ref, slot_ref, feats_hbm, cot_hbm, w_hbm, w_upd_hbm,
                 ent_out_ref, fact_grad_hbm, left_out_ref, side_out_ref, *scratch):
    bf16, f32 = jnp.bfloat16, jnp.float32
    here = position()
    ent, rep = lax.axis_index("ent"), lax.axis_index("rep")
    n_rep = grid[R_HI] * grid[R_LO]
    greeted = greet(grid, here)
    scratch = list(scratch)

    def take(number):
        taken, scratch[:number] = scratch[:number], []
        return taken

    facts_ref, feats_ref, cot_ref, w_ref, w_upd_ref, in_sems, out_sems = take(7)
    pos_ref, gate_ref, d_pre_ref, spread_ref, hot_ref, hot_t, facts_t, w_t, w_upd_t = take(9)
    parts, parts_sent, all_refs = take(CHUNKS), take(CHUNKS), take(CHUNKS)
    count_ref, mean_ref, grad_z_ref = take(3)
    side_ref, side_sent, left_ref, left_sent = take(4)
    message_ref = d_pre_ref
    fact_rows, width = facts_ref.shape
    half = width // 2
    halves = [slice(0, half), slice(half, width)]
    every = (slice(None),) * 5
    piece = parts[0].shape[-2]
    share = piece * CHUNKS
    ent_rows = share * n_rep
    n_ents = ent_rows * grid[E_HI] * grid[E_LO]
    chunk = n_ents // CHUNKS
    block = fact_rows // 4
    rows_step = 4 * n_rep * piece
    orders = (ORDER_A, ORDER_B)

    counts = Counts(grid, here, ORDER_A, count_ref, take(16))
    sums = [Scatter(grid, here, orders[c], parts[c], parts_sent[c], take(20)) for c in range(CHUNKS)]
    spreads = [
        Gather(grid, here, ALL, orders[c][::-1], all_refs[c], take(8)) for c in range(CHUNKS)
    ]
    sides = Scatter(grid, here, ORDER_A, side_ref, side_sent, take(20))
    lefts = [
        Scatter(grid, here, order, left_ref.at[every + (cols,)], left_sent.at[every + (cols,)],
                take(20))
        for order, cols in zip(orders, halves)
    ]
    ent_spread = Gather(grid, here, (R_HI, R_LO), (R_HI, R_LO), ent_out_ref, take(4))

    def facts_copy(step):
        rows = pl.ds(pl.multiple_of(step * block, block), block)
        return pltpu.make_async_copy(facts_hbm.at[rows, :], facts_ref.at[rows, :], in_sems.at[step])

    others = [
        pltpu.make_async_copy(source, target, in_sems.at[4 + index])
        for index, (source, target) in enumerate([
            (w_hbm, w_ref), (w_upd_hbm, w_upd_ref), (cot_hbm, cot_ref), (feats_hbm, feats_ref)
        ])
    ]
    others[0].start()
    for step in range(4):
        facts_copy(step).start()
    for copy in others[1:]:
        copy.start()

    slot = slot_ref[...]
    pos_ref[...] = (
        lax.rem(slot, share) // piece * chunk
        + (owner_ref[...] * n_rep + slot // share) * piece
        + lax.rem(slot, piece)
    )
    others[0].wait()

    def project(step, carry):
        facts_copy(step).wait()
        rows = pl.ds(pl.multiple_of(step * block, block), block)
        pre = jnp.dot(facts_ref[rows, :], w_ref[...], preferred_element_type=f32)
        sig = jax.nn.sigmoid(pre)
        gate_ref[rows, :] = sig * (1.0 + pre * (1.0 - sig))
        message_ref[rows, :] = (pre * sig).astype(bf16)
        return carry

    lax.fori_loop(0, 4, project, 0)

    for c in range(CHUNKS):

        def gather_sums(step, carry, c=c):
            first = c * chunk + step * rows_step
            ids = lax.broadcasted_iota(jnp.int32, (rows_step, fact_rows), 0) + first
            hit = (ids == pos_ref[...]).astype(f32)
            hot = hit.astype(bf16)
            total = jnp.sum(hit, axis=1, keepdims=True)
            for low in range(rows_step // 128):
                column = jnp.broadcast_to(total[low * 128:(low + 1) * 128], (128, 128))
                count_ref[pl.ds(first // 128 + low, 1), :] = jnp.transpose(column)[0:1, :]
            agg = jnp.dot(hot, message_ref[...], preferred_element_type=f32)
            agg = agg.reshape(2, 2, grid[R_HI], 2, piece, width)
            parts[c][pl.ds(step * 2, 2)] = agg
            parts_sent[c][pl.ds(step * 2, 2)] = agg.astype(bf16)
            return carry

        lax.fori_loop(0, grid[E_HI] // 2, gather_sums, 0)
        if c == 0:
            pl.semaphore_wait(pltpu.get_barrier_semaphore(), greeted)
        sums[c].start()
    counts.start()

    def turn_facts(step, carry):
        rows = pl.ds(pl.multiple_of(step * block, block), block)
        facts_t[:, rows] = jnp.transpose(facts_ref[rows, :])
        return carry

    def hits_of(step, c):
        keys = jnp.concatenate([
            jnp.transpose(jnp.broadcast_to(
                pos_ref[:, pl.ds(pl.multiple_of(step * block + at, 128), 128)], (128, 128)
            ))
            for at in range(0, block, 128)
        ], axis=0)
        return jnp.concatenate([
            (keys == lax.broadcasted_iota(jnp.int32, (block, 128), 1) + (c * chunk + at))
            .astype(f32).astype(bf16)
            for at in range(0, chunk, 128)
        ], axis=1)

    def turn_hits(step, carry):
        rows = pl.ds(pl.multiple_of(step * block, block), block)
        for c in range(CHUNKS):
            hot_t[rows, c * chunk:(c + 1) * chunk] = hits_of(step, c)
        return carry

    def hits(step, c):
        if not kept:
            return hits_of(step, c)
        rows = pl.ds(pl.multiple_of(step * block, block), block)
        return hot_t[rows, c * chunk:(c + 1) * chunk]

    counts.advance()
    for item in sums:
        item.advance()
    for copy in others[1:]:
        copy.wait()
    w_upd_t[...] = jnp.transpose(w_upd_ref[...])
    w_t[...] = jnp.transpose(w_ref[...])
    lax.fori_loop(0, 4, turn_facts, 0)
    counts.advance()
    for item in sums:
        item.advance()
    if kept:
        lax.fori_loop(0, 4, turn_hits, 0)
    counts.advance()
    for item in sums:
        item.advance()
    counts.advance()

    def entity(c):
        first = c * chunk + (ent * n_rep + rep) * piece
        table = counts.table[...]
        line = jnp.sum(
            jnp.where(
                lax.broadcasted_iota(jnp.int32, table.shape, 0) == first // 128, table, 0.0
            ), axis=0, keepdims=True,
        )
        lane = lax.broadcasted_iota(jnp.int32, (piece, 128), 1)
        row = lax.broadcasted_iota(jnp.int32, (piece, 128), 0) + lax.rem(first, 128)
        count = jnp.sum(
            jnp.where(lane == row, jnp.broadcast_to(line, (piece, 128)), 0.0),
            axis=1, keepdims=True,
        )
        denom = jnp.maximum(count, 1.0)
        rows = slice(c * piece, (c + 1) * piece)
        mean = (sums[c].own[...] / denom).astype(bf16)
        zval = jnp.dot(mean, w_upd_ref[...], preferred_element_type=f32)
        grad_z = (cot_ref[rep, rows].astype(f32) * silu_grad(zval)).astype(bf16)
        d_mean = jnp.dot(grad_z, w_upd_t[...], preferred_element_type=f32)
        all_refs[c][here] = (d_mean / denom).astype(bf16)
        spreads[c].start()
        mean_ref[rows, :] = mean
        grad_z_ref[rows, :] = grad_z
        value = feats_ref[rep, rows].astype(f32) + zval * jax.nn.sigmoid(zval)
        ent_out_ref[here[R_HI], here[R_LO], rows] = value.astype(bf16)

    for c in range(CHUNKS):
        sums[c].advance()
        entity(c)

    side = lax.dot_general(
        grad_z_ref[...], mean_ref[...], (((0,), (0,)), ((), ())), preferred_element_type=f32
    )
    side_ref[...] = side.reshape(side_ref.shape)
    side_sent[...] = side.astype(bf16).reshape(side_ref.shape)
    sides.start()
    for stage in range(3):
        for item in spreads:
            item.advance()
    sides.finish()

    def expand_first(step, carry):
        rows = pl.ds(pl.multiple_of(step * block, block), block)
        spread_ref[rows, :] = jnp.dot(
            hits(step, 0), all_refs[0][...].reshape(chunk, width), preferred_element_type=f32
        )
        return carry

    spreads[0].advance()
    sides.start()
    ent_spread.start()
    lax.fori_loop(0, 4, expand_first, 0)
    spreads[1].advance()

    for number, cols in enumerate(halves):

        def expand(step, carry, cols=cols):
            rows = pl.ds(pl.multiple_of(step * block, block), block)
            table = all_refs[1][every + (cols,)].reshape(chunk, half)
            d_msg = spread_ref[rows, cols] + jnp.dot(
                hits(step, 1), table, preferred_element_type=f32
            )
            d_pre_ref[rows, cols] = (d_msg * gate_ref[rows, cols]).astype(bf16)
            return carry

        lax.fori_loop(0, 4, expand, 0)
        left = jnp.dot(facts_t[...], d_pre_ref[:, cols], preferred_element_type=f32)
        left = left.reshape(left_ref.shape[:-1] + (half,))
        left_ref[every + (cols,)] = left
        left_sent[every + (cols,)] = left.astype(bf16)
        lefts[number].start()
    sides.advance()
    ent_spread.advance()
    for item in lefts:
        item.advance()

    grad_ref = facts_ref

    def grad_copy(step):
        rows = pl.ds(pl.multiple_of(step * block, block), block)
        return pltpu.make_async_copy(
            grad_ref.at[rows, :], fact_grad_hbm.at[rows, :], out_sems.at[step]
        )

    def fact_grads(step, carry):
        rows = pl.ds(pl.multiple_of(step * block, block), block)
        grad_ref[rows, :] = jnp.dot(
            d_pre_ref[rows, :], w_t[...], preferred_element_type=f32
        ).astype(bf16)
        grad_copy(step).start()
        return carry

    lax.fori_loop(0, 4, fact_grads, 0)
    sides.advance()
    ent_spread.advance()
    for item in lefts:
        item.advance()
    sides.advance()
    side_out_ref[...] = sides.own[...]
    for item in lefts:
        item.advance()
    for step in range(4):
        grad_copy(step).wait()
    for item in lefts:
        item.advance()
    left_out_ref[:, 0:half] = lefts[0].own[...]
    left_out_ref[:, half:width] = lefts[1].own[...]


def in_vmem(number):
    return [pl.BlockSpec(memory_space=pltpu.VMEM)] * number


def anywhere(number):
    return [pl.BlockSpec(memory_space=pl.ANY)] * number


def per_device(facts, fact_owner, fact_slot, entity_feats, out_cotangent, w_msg, w_upd):
    n_owners = lax.axis_size("ent")
    n_copies = lax.axis_size("rep")
    grid = (n_owners // 2, 2, n_copies // 2, 2)
    fact_rows, width = facts.shape
    ent_rows = entity_feats.shape[0]
    ents = ent_rows * n_owners
    share = ent_rows // n_copies
    piece = share // CHUNKS
    bf16, f32 = jnp.bfloat16, jnp.float32
    rows = width // (n_owners * n_copies)
    half = width // 2
    kept = ents <= 1024
    table = (ents // 128, 128)
    orders = (ORDER_A, ORDER_B)
    ent_out, fact_grad, left, side = pl.pallas_call(
        functools.partial(layer_kernel, grid, kept),
        out_shape=(
            jax.ShapeDtypeStruct((grid[R_HI], grid[R_LO], share, width), bf16),
            jax.ShapeDtypeStruct((fact_rows, width), bf16),
            jax.ShapeDtypeStruct((rows, width), f32),
            jax.ShapeDtypeStruct((rows, width), f32),
        ),
        in_specs=anywhere(1) + in_vmem(2) + anywhere(4),
        out_specs=in_vmem(1) + anywhere(1) + in_vmem(2),
        scratch_shapes=(
            [
                pltpu.VMEM((fact_rows, width), bf16),
                pltpu.VMEM((n_copies, share, width), bf16),
                pltpu.VMEM((n_copies, share, width), bf16),
                pltpu.VMEM((width, width), bf16),
                pltpu.VMEM((width, width), bf16),
                pltpu.SemaphoreType.DMA((8,)),
                pltpu.SemaphoreType.DMA((4,)),
                pltpu.VMEM((1, fact_rows), jnp.int32),
                pltpu.VMEM((fact_rows, width), f32),
                pltpu.VMEM((fact_rows, width), bf16),
                pltpu.VMEM((fact_rows, width), f32),
                pltpu.VMEM((16, 128), bf16),
                pltpu.VMEM((fact_rows, ents) if kept else (16, 128), bf16),
                pltpu.VMEM((width, fact_rows), bf16),
                pltpu.VMEM((width, width), bf16),
                pltpu.VMEM((width, width), bf16),
            ]
            + [pltpu.VMEM(grid + (piece, width), f32)] * CHUNKS
            + [pltpu.VMEM(grid + (piece, width), bf16)] * (2 * CHUNKS)
            + [
                pltpu.VMEM(table, f32),
                pltpu.VMEM((share, width), bf16),
                pltpu.VMEM((share, width), bf16),
            ]
            + [
                pltpu.VMEM(grid + (rows, width), f32),
                pltpu.VMEM(grid + (rows, width), bf16),
            ] * 2
            + count_scratch(grid, ORDER_A, table)
            + sum_scratch(grid, ORDER_A, (piece, width), bf16)
            + sum_scratch(grid, ORDER_B, (piece, width), bf16)
            + gather_scratch(grid, ORDER_A[::-1])
            + gather_scratch(grid, ORDER_B[::-1])
            + sum_scratch(grid, ORDER_A, (rows, width), bf16)
            + sum_scratch(grid, ORDER_A, (rows, half), bf16)
            + sum_scratch(grid, ORDER_B, (rows, half), bf16)
            + gather_scratch(grid, (R_HI, R_LO))
        ),
        compiler_params=pltpu.CompilerParams(
            collective_id=0, has_side_effects=True, vmem_limit_bytes=VMEM_LIMIT
        ),
    )(
        facts,
        fact_owner.reshape(1, fact_rows),
        fact_slot.reshape(1, fact_rows),
        entity_feats.reshape(n_copies, share, width),
        out_cotangent.reshape(n_copies, share, width),
        w_msg,
        w_upd,
    )
    return (ent_out.reshape(ent_rows, width), fact_grad, left, side)


def solution(mesh):
    placed = (
        P(("ent", "rep"), None),
        P(("ent", "rep"), None),
        P(("ent", "rep")),
        P("ent", None),
        P("ent", None),
        P(),
        P(),
    )
    return jax.shard_map(
        per_device,
        mesh=mesh,
        in_specs=placed,
        out_specs=(
            P("ent", None),
            P(("ent", "rep"), None),
            P(("ent", "rep"), None),
            P(("ent", "rep"), None),
        ),
        check_vma=False,
    )
```

```python
import functools

import jax
import jax.numpy as jnp
from jax import lax
from jax.experimental import pallas as pl
from jax.experimental.pallas import tpu as pltpu
from jax.sharding import PartitionSpec as P

E_HI, E_LO, R_HI, R_LO = range(4)
ALL = (E_HI, E_LO, R_HI, R_LO)
ORDER_A = (R_LO, R_HI, E_LO, E_HI)
ORDER_B = (R_LO, E_LO, R_HI, E_HI)
MESH = pl.DeviceIdType.MESH
CHUNKS = 2


def silu_grad(value):
    sig = jax.nn.sigmoid(value)
    return sig * (1.0 + value * (1.0 - sig))


def position():
    ent, rep = lax.axis_index("ent"), lax.axis_index("rep")
    return (ent // 2, lax.rem(ent, 2), rep // 2, lax.rem(rep, 2))


def device_at(here, dim, coord):
    if dim == E_HI:
        return {"ent": coord * 2 + here[E_LO]}
    if dim == E_LO:
        return {"ent": here[E_HI] * 2 + coord}
    if dim == R_HI:
        return {"rep": coord * 2 + here[R_LO]}
    return {"rep": here[R_HI] * 2 + coord}


def greet(grid, here):
    barrier = pltpu.get_barrier_semaphore()
    total = 0
    for dim in ALL:
        for step in range(1, grid[dim]):
            target = device_at(here, dim, lax.rem(here[dim] + step, grid[dim]))
            pl.semaphore_signal(barrier, inc=1, device_id=target, device_id_type=MESH)
            total += 1
    return total


def sum_scratch(grid, order, tail, dtype):
    left, shapes = [0, 1, 2, 3], []
    for dim in order:
        left.remove(dim)
        kept = tuple(grid[d] for d in left) + tail
        shapes += [
            pltpu.VMEM((grid[dim] - 1,) + kept, dtype),
            pltpu.VMEM(kept, jnp.float32),
            pltpu.VMEM(kept if left else (16, 128), dtype),
            pltpu.SemaphoreType.DMA((grid[dim] - 1,)),
            pltpu.SemaphoreType.DMA((grid[dim] - 1,)),
        ]
    return shapes


class Scatter:
    def __init__(self, grid, here, order, own, sent, scratch):
        self.grid, self.here, self.order, self.own, self.sent = grid, here, order, own, sent
        self.scratch, self.left, self.stage = scratch, [0, 1, 2, 3], 0

    def start(self):
        dim = self.order[self.stage]
        size, mine = self.grid[dim], self.here[dim]
        arrived, _, _, send, recv = self.scratch[5 * self.stage:5 * self.stage + 5]
        lead = (slice(None),) * self.left.index(dim)
        self.copies = []
        for step in range(1, size):
            coord = lax.rem(mine + step, size)
            copy = pltpu.make_async_remote_copy(
                src_ref=self.sent.at[lead + (coord,)],
                dst_ref=arrived.at[step - 1],
                send_sem=send.at[step - 1],
                recv_sem=recv.at[step - 1],
                device_id=device_at(self.here, dim, coord),
                device_id_type=MESH,
            )
            copy.start()
            self.copies.append(copy)

    def finish(self):
        dim = self.order[self.stage]
        arrived, total, rounded, _, _ = self.scratch[5 * self.stage:5 * self.stage + 5]
        lead = (slice(None),) * self.left.index(dim)
        value = self.own[lead + (self.here[dim],)]
        for index, copy in enumerate(self.copies):
            copy.wait()
            value = value + arrived[index].astype(jnp.float32)
        total[...] = value
        self.own = self.sent = total
        self.left.remove(dim)
        self.stage += 1
        if self.left and rounded.dtype != jnp.float32:
            rounded[...] = value.astype(rounded.dtype)
            self.sent = rounded

    def advance(self):
        self.finish()
        if self.stage < 4:
            self.start()


class Counts:
    def __init__(self, grid, here, order, table, scratch):
        self.grid, self.here, self.order, self.table = grid, here, order, table
        self.scratch, self.stage = scratch, 0

    def start(self):
        dim = self.order[self.stage]
        size, mine = self.grid[dim], self.here[dim]
        arrived, _, send, recv = self.scratch[4 * self.stage:4 * self.stage + 4]
        self.copies = []
        for step in range(1, size):
            copy = pltpu.make_async_remote_copy(
                src_ref=self.table,
                dst_ref=arrived.at[step - 1],
                send_sem=send.at[step - 1],
                recv_sem=recv.at[step - 1],
                device_id=device_at(self.here, dim, lax.rem(mine + step, size)),
                device_id_type=MESH,
            )
            copy.start()
            self.copies.append(copy)

    def advance(self):
        arrived, total, _, _ = self.scratch[4 * self.stage:4 * self.stage + 4]
        value = self.table[...]
        for index, copy in enumerate(self.copies):
            copy.wait()
            value = value + arrived[index]
        total[...] = value
        self.table = total
        self.stage += 1
        if self.stage < 4:
            self.start()


def count_scratch(grid, order, tail):
    shapes = []
    for dim in order:
        shapes += [
            pltpu.VMEM((grid[dim] - 1,) + tail, jnp.float32),
            pltpu.VMEM(tail, jnp.float32),
            pltpu.SemaphoreType.DMA((grid[dim] - 1,)),
            pltpu.SemaphoreType.DMA((grid[dim] - 1,)),
        ]
    return shapes


class Gather:
    def __init__(self, grid, here, dims, order, ref, sems):
        self.grid, self.here, self.dims, self.order = grid, here, dims, order
        self.ref, self.sems = ref, sems
        self.done, self.stage = [], 0

    def start(self):
        dim = self.order[self.stage]
        size, mine = self.grid[dim], self.here[dim]
        send, recv = self.sems[2 * self.stage:2 * self.stage + 2]
        index = tuple(slice(None) if d in self.done else self.here[d] for d in self.dims)
        block = self.ref.at[index]
        self.copies = []
        for step in range(1, size):
            coord = lax.rem(mine + step, size)
            copy = pltpu.make_async_remote_copy(
                src_ref=block,
                dst_ref=block,
                send_sem=send.at[step - 1],
                recv_sem=recv.at[step - 1],
                device_id=device_at(self.here, dim, coord),
                device_id_type=MESH,
            )
            copy.start()
            self.copies.append(copy)

    def advance(self):
        for copy in self.copies:
            copy.wait()
        self.done.append(self.order[self.stage])
        self.stage += 1
        if self.stage < len(self.order):
            self.start()


def gather_scratch(grid, order):
    return [pltpu.SemaphoreType.DMA((grid[d] - 1,)) for d in order for _ in range(2)]


def layer_kernel(grid, kept, facts_hbm, owner_ref, slot_ref, feats_hbm, cot_hbm, w_hbm, w_upd_hbm,
                 ent_out_ref, fact_grad_hbm, left_out_ref, side_out_ref, *scratch):
    bf16, f32 = jnp.bfloat16, jnp.float32
    here = position()
    ent, rep = lax.axis_index("ent"), lax.axis_index("rep")
    n_rep = grid[R_HI] * grid[R_LO]
    greeted = greet(grid, here)
    scratch = list(scratch)

    def take(number):
        taken, scratch[:number] = scratch[:number], []
        return taken

    facts_ref, feats_ref, cot_ref, w_ref, w_upd_ref, in_sems, out_sems = take(7)
    pos_ref, gate_ref, d_pre_ref, spread_ref, hot_ref, hot_t, facts_t, w_t, w_upd_t = take(9)
    parts, parts_sent, all_refs = take(CHUNKS), take(CHUNKS), take(CHUNKS)
    count_ref, mean_ref, grad_z_ref = take(3)
    side_ref, side_sent, left_ref, left_sent = take(4)
    message_ref = d_pre_ref
    fact_rows, width = facts_ref.shape
    half = width // 2
    halves = [slice(0, half), slice(half, width)]
    every = (slice(None),) * 5
    piece = parts[0].shape[-2]
    share = piece * CHUNKS
    ent_rows = share * n_rep
    n_ents = ent_rows * grid[E_HI] * grid[E_LO]
    chunk = n_ents // CHUNKS
    block = fact_rows // 4
    rows_step = 4 * n_rep * piece
    orders = (ORDER_A, ORDER_B)

    counts = Counts(grid, here, ORDER_A, count_ref, take(16))
    sums = [Scatter(grid, here, orders[c], parts[c], parts_sent[c], take(20)) for c in range(CHUNKS)]
    spreads = [
        Gather(grid, here, ALL, orders[c][::-1], all_refs[c], take(8)) for c in range(CHUNKS)
    ]
    sides = Scatter(grid, here, ORDER_A, side_ref, side_sent, take(20))
    lefts = [
        Scatter(grid, here, order, left_ref.at[every + (cols,)], left_sent.at[every + (cols,)],
                take(20))
        for order, cols in zip(orders, halves)
    ]
    ent_spread = Gather(grid, here, (R_HI, R_LO), (R_HI, R_LO), ent_out_ref, take(4))

    def facts_copy(step):
        rows = pl.ds(pl.multiple_of(step * block, block), block)
        return pltpu.make_async_copy(facts_hbm.at[rows, :], facts_ref.at[rows, :], in_sems.at[step])

    others = [
        pltpu.make_async_copy(source, target, in_sems.at[4 + index])
        for index, (source, target) in enumerate([
            (w_hbm, w_ref), (w_upd_hbm, w_upd_ref), (cot_hbm, cot_ref), (feats_hbm, feats_ref)
        ])
    ]
    others[0].start()
    for step in range(4):
        facts_copy(step).start()
    for copy in others[1:]:
        copy.start()

    slot = slot_ref[...]
    pos_ref[...] = (
        lax.rem(slot, share) // piece * chunk
        + (owner_ref[...] * n_rep + slot // share) * piece
        + lax.rem(slot, piece)
    )
    others[0].wait()

    def project(step, carry):
        facts_copy(step).wait()
        rows = pl.ds(pl.multiple_of(step * block, block), block)
        pre = jnp.dot(facts_ref[rows, :], w_ref[...], preferred_element_type=f32)
        sig = jax.nn.sigmoid(pre)
        gate_ref[rows, :] = sig * (1.0 + pre * (1.0 - sig))
        message_ref[rows, :] = (pre * sig).astype(bf16)
        return carry

    lax.fori_loop(0, 4, project, 0)

    for c in range(CHUNKS):

        def gather_sums(step, carry, c=c):
            first = c * chunk + step * rows_step
            ids = lax.broadcasted_iota(jnp.int32, (rows_step, fact_rows), 0) + first
            hit = (ids == pos_ref[...]).astype(f32)
            hot = hit.astype(bf16)
            total = jnp.sum(hit, axis=1, keepdims=True)
            for low in range(rows_step // 128):
                column = jnp.broadcast_to(total[low * 128:(low + 1) * 128], (128, 128))
                count_ref[pl.ds(first // 128 + low, 1), :] = jnp.transpose(column)[0:1, :]
            agg = jnp.dot(hot, message_ref[...], preferred_element_type=f32)
            agg = agg.reshape(2, 2, grid[R_HI], 2, piece, width)
            parts[c][pl.ds(step * 2, 2)] = agg
            parts_sent[c][pl.ds(step * 2, 2)] = agg.astype(bf16)
            return carry

        lax.fori_loop(0, grid[E_HI] // 2, gather_sums, 0)
        if c == 0:
            pl.semaphore_wait(pltpu.get_barrier_semaphore(), greeted)
        sums[c].start()
    counts.start()

    def turn_facts(step, carry):
        rows = pl.ds(pl.multiple_of(step * block, block), block)
        facts_t[:, rows] = jnp.transpose(facts_ref[rows, :])
        return carry

    def hits_of(step, c):
        keys = jnp.concatenate([
            jnp.transpose(jnp.broadcast_to(
                pos_ref[:, pl.ds(pl.multiple_of(step * block + at, 128), 128)], (128, 128)
            ))
            for at in range(0, block, 128)
        ], axis=0)
        return jnp.concatenate([
            (keys == lax.broadcasted_iota(jnp.int32, (block, 128), 1) + (c * chunk + at))
            .astype(f32).astype(bf16)
            for at in range(0, chunk, 128)
        ], axis=1)

    def turn_hits(step, carry):
        rows = pl.ds(pl.multiple_of(step * block, block), block)
        for c in range(CHUNKS):
            hot_t[rows, c * chunk:(c + 1) * chunk] = hits_of(step, c)
        return carry

    def hits(step, c):
        if not kept:
            return hits_of(step, c)
        rows = pl.ds(pl.multiple_of(step * block, block), block)
        return hot_t[rows, c * chunk:(c + 1) * chunk]

    counts.advance()
    for item in sums:
        item.advance()
    for copy in others[1:]:
        copy.wait()
    w_upd_t[...] = jnp.transpose(w_upd_ref[...])
    w_t[...] = jnp.transpose(w_ref[...])
    lax.fori_loop(0, 4, turn_facts, 0)
    counts.advance()
    for item in sums:
        item.advance()
    if kept:
        lax.fori_loop(0, 4, turn_hits, 0)
    counts.advance()
    for item in sums:
        item.advance()
    counts.advance()

    def entity(c):
        first = c * chunk + (ent * n_rep + rep) * piece
        table = counts.table[...]
        line = jnp.sum(
            jnp.where(
                lax.broadcasted_iota(jnp.int32, table.shape, 0) == first // 128, table, 0.0
            ), axis=0, keepdims=True,
        )
        lane = lax.broadcasted_iota(jnp.int32, (piece, 128), 1)
        row = lax.broadcasted_iota(jnp.int32, (piece, 128), 0) + lax.rem(first, 128)
        count = jnp.sum(
            jnp.where(lane == row, jnp.broadcast_to(line, (piece, 128)), 0.0),
            axis=1, keepdims=True,
        )
        denom = jnp.maximum(count, 1.0)
        rows = slice(c * piece, (c + 1) * piece)
        mean = (sums[c].own[...] / denom).astype(bf16)
        zval = jnp.dot(mean, w_upd_ref[...], preferred_element_type=f32)
        grad_z = (cot_ref[rep, rows].astype(f32) * silu_grad(zval)).astype(bf16)
        d_mean = jnp.dot(grad_z, w_upd_t[...], preferred_element_type=f32)
        all_refs[c][here] = (d_mean / denom).astype(bf16)
        spreads[c].start()
        mean_ref[rows, :] = mean
        grad_z_ref[rows, :] = grad_z
        value = feats_ref[rep, rows].astype(f32) + zval * jax.nn.sigmoid(zval)
        ent_out_ref[here[R_HI], here[R_LO], rows] = value.astype(bf16)

    for c in range(CHUNKS):
        sums[c].advance()
        entity(c)

    side = lax.dot_general(
        grad_z_ref[...], mean_ref[...], (((0,), (0,)), ((), ())), preferred_element_type=f32
    )
    side_ref[...] = side.reshape(side_ref.shape)
    side_sent[...] = side.astype(bf16).reshape(side_ref.shape)
    sides.start()
    for stage in range(3):
        for item in spreads:
            item.advance()
    sides.finish()

    def expand_first(step, carry):
        rows = pl.ds(pl.multiple_of(step * block, block), block)
        spread_ref[rows, :] = jnp.dot(
            hits(step, 0), all_refs[0][...].reshape(chunk, width), preferred_element_type=f32
        )
        return carry

    spreads[0].advance()
    sides.start()
    ent_spread.start()
    lax.fori_loop(0, 4, expand_first, 0)
    spreads[1].advance()

    for number, cols in enumerate(halves):

        def expand(step, carry, cols=cols):
            rows = pl.ds(pl.multiple_of(step * block, block), block)
            table = all_refs[1][every + (cols,)].reshape(chunk, half)
            d_msg = spread_ref[rows, cols] + jnp.dot(
                hits(step, 1), table, preferred_element_type=f32
            )
            d_pre_ref[rows, cols] = (d_msg * gate_ref[rows, cols]).astype(bf16)
            return carry

        lax.fori_loop(0, 4, expand, 0)
        left = jnp.dot(facts_t[...], d_pre_ref[:, cols], preferred_element_type=f32)
        left = left.reshape(left_ref.shape[:-1] + (half,))
        left_ref[every + (cols,)] = left
        left_sent[every + (cols,)] = left.astype(bf16)
        lefts[number].start()
    sides.advance()
    ent_spread.advance()
    for item in lefts:
        item.advance()

    grad_ref = facts_ref

    def grad_copy(step):
        rows = pl.ds(pl.multiple_of(step * block, block), block)
        return pltpu.make_async_copy(
            grad_ref.at[rows, :], fact_grad_hbm.at[rows, :], out_sems.at[step]
        )

    def fact_grads(step, carry):
        rows = pl.ds(pl.multiple_of(step * block, block), block)
        grad_ref[rows, :] = jnp.dot(
            d_pre_ref[rows, :], w_t[...], preferred_element_type=f32
        ).astype(bf16)
        grad_copy(step).start()
        return carry

    lax.fori_loop(0, 4, fact_grads, 0)
    sides.advance()
    ent_spread.advance()
    for item in lefts:
        item.advance()
    sides.advance()
    side_out_ref[...] = sides.own[...]
    for item in lefts:
        item.advance()
    for step in range(4):
        grad_copy(step).wait()
    for item in lefts:
        item.advance()
    left_out_ref[:, 0:half] = lefts[0].own[...]
    left_out_ref[:, half:width] = lefts[1].own[...]


def write_kernel(*refs):
    count = (len(refs) - 1) // 2
    sources, targets, sems = refs[:count], refs[count:2 * count], refs[-1]
    copies = []
    for source, target in zip(sources, targets):
        pieces = 4 if source.shape[0] % 64 == 0 and source.shape[0] > 1024 else 1
        rows = source.shape[0] // pieces
        for piece in range(pieces):
            at = pl.ds(piece * rows, rows)
            copies.append(
                pltpu.make_async_copy(source.at[at], target.at[at], sems.at[len(copies)])
            )
    for copy in copies:
        copy.start()
    for copy in copies:
        copy.wait()


def in_vmem(number):
    return [pl.BlockSpec(memory_space=pltpu.VMEM)] * number


def anywhere(number):
    return [pl.BlockSpec(memory_space=pl.ANY)] * number


def in_hbm(number):
    return [pl.BlockSpec(memory_space=pltpu.HBM)] * number


def per_device(facts, fact_owner, fact_slot, entity_feats, out_cotangent, w_msg, w_upd):
    n_owners = lax.axis_size("ent")
    n_copies = lax.axis_size("rep")
    grid = (n_owners // 2, 2, n_copies // 2, 2)
    fact_rows, width = facts.shape
    ent_rows = entity_feats.shape[0]
    ents = ent_rows * n_owners
    share = ent_rows // n_copies
    piece = share // CHUNKS
    bf16, f32 = jnp.bfloat16, jnp.float32
    rows = width // (n_owners * n_copies)
    half = width // 2
    kept = ents <= 1024
    table = (ents // 128, 128)
    orders = (ORDER_A, ORDER_B)
    ent_out, fact_grad, left, side = pl.pallas_call(
        functools.partial(layer_kernel, grid, kept),
        out_shape=(
            jax.ShapeDtypeStruct((grid[R_HI], grid[R_LO], share, width), bf16),
            jax.ShapeDtypeStruct((fact_rows, width), bf16),
            jax.ShapeDtypeStruct((rows, width), f32),
            jax.ShapeDtypeStruct((rows, width), f32),
        ),
        in_specs=in_hbm(1) + in_vmem(2) + in_hbm(4),
        out_specs=in_vmem(1) + anywhere(1) + in_vmem(2),
        scratch_shapes=(
            [
                pltpu.VMEM((fact_rows, width), bf16),
                pltpu.VMEM((n_copies, share, width), bf16),
                pltpu.VMEM((n_copies, share, width), bf16),
                pltpu.VMEM((width, width), bf16),
                pltpu.VMEM((width, width), bf16),
                pltpu.SemaphoreType.DMA((8,)),
                pltpu.SemaphoreType.DMA((4,)),
                pltpu.VMEM((1, fact_rows), jnp.int32),
                pltpu.VMEM((fact_rows, width), f32),
                pltpu.VMEM((fact_rows, width), bf16),
                pltpu.VMEM((fact_rows, width), f32),
                pltpu.VMEM((16, 128), bf16),
                pltpu.VMEM((fact_rows, ents) if kept else (16, 128), bf16),
                pltpu.VMEM((width, fact_rows), bf16),
                pltpu.VMEM((width, width), bf16),
                pltpu.VMEM((width, width), bf16),
            ]
            + [pltpu.VMEM(grid + (piece, width), f32)] * CHUNKS
            + [pltpu.VMEM(grid + (piece, width), bf16)] * (2 * CHUNKS)
            + [
                pltpu.VMEM(table, f32),
                pltpu.VMEM((share, width), bf16),
                pltpu.VMEM((share, width), bf16),
            ]
            + [
                pltpu.VMEM(grid + (rows, width), f32),
                pltpu.VMEM(grid + (rows, width), bf16),
            ] * 2
            + count_scratch(grid, ORDER_A, table)
            + sum_scratch(grid, ORDER_A, (piece, width), bf16)
            + sum_scratch(grid, ORDER_B, (piece, width), bf16)
            + gather_scratch(grid, ORDER_A[::-1])
            + gather_scratch(grid, ORDER_B[::-1])
            + sum_scratch(grid, ORDER_A, (rows, width), bf16)
            + sum_scratch(grid, ORDER_A, (rows, half), bf16)
            + sum_scratch(grid, ORDER_B, (rows, half), bf16)
            + gather_scratch(grid, (R_HI, R_LO))
        ),
        compiler_params=pltpu.CompilerParams(
            collective_id=0, has_side_effects=True, vmem_limit_bytes=(48 if kept else 60) << 20
        ),
    )(*[
        pltpu.with_memory_space_constraint(operand, pltpu.HBM)
        for operand in (
            facts,
            fact_owner.reshape(1, fact_rows),
            fact_slot.reshape(1, fact_rows),
            entity_feats.reshape(n_copies, share, width),
            out_cotangent.reshape(n_copies, share, width),
            w_msg,
            w_upd,
        )
    ])
    results = (ent_out.reshape(ent_rows, width), fact_grad, left, side)
    return pl.pallas_call(
        write_kernel,
        out_shape=tuple(jax.ShapeDtypeStruct(r.shape, r.dtype) for r in results),
        in_specs=anywhere(4),
        out_specs=in_hbm(4),
        scratch_shapes=[pltpu.SemaphoreType.DMA((8,))],
        compiler_params=pltpu.CompilerParams(vmem_limit_bytes=4 << 20),
    )(*results)


def solution(mesh):
    placed = (
        P(("ent", "rep"), None),
        P(("ent", "rep"), None),
        P(("ent", "rep")),
        P("ent", None),
        P("ent", None),
        P(),
        P(),
    )
    return jax.shard_map(
        per_device,
        mesh=mesh,
        in_specs=placed,
        out_specs=(
            P("ent", None),
            P(("ent", "rep"), None),
            P(("ent", "rep"), None),
            P(("ent", "rep"), None),
        ),
        check_vma=False,
    )
```

```python
import functools
import math

import jax
import jax.numpy as jnp
from jax import lax
from jax.experimental import pallas as pl
from jax.experimental.pallas import tpu as pltpu
from jax.sharding import PartitionSpec as P

E_HI, E_LO, R_HI, R_LO = range(4)
STAGES = ((R_LO,), (R_HI, E_LO), (E_HI,))
MESH = pl.DeviceIdType.MESH
CHUNKS = 2


def silu_grad(value):
    sig = jax.nn.sigmoid(value)
    return sig * (1.0 + value * (1.0 - sig))


def position():
    ent, rep = lax.axis_index("ent"), lax.axis_index("rep")
    return (ent // 2, lax.rem(ent, 2), rep // 2, lax.rem(rep, 2))


def peers_of(grid, here, dims):
    offsets = [()]
    for dim in dims:
        offsets = [offset + (step,) for offset in offsets for step in range(grid[dim])]
    offsets = sorted(offsets[1:], key=lambda offset: -sum(step > 0 for step in offset))
    places = []
    for offset in offsets:
        place = list(here)
        for dim, step in zip(dims, offset):
            place[dim] = lax.rem(here[dim] + step, grid[dim])
        places.append(tuple(place))
    return places


def peer_count(grid, dims):
    return math.prod(grid[dim] for dim in dims) - 1


def device_id(place):
    return {"ent": place[E_HI] * 2 + place[E_LO], "rep": place[R_HI] * 2 + place[R_LO]}


def send_to(place, source, target, send_sem, recv_sem):
    copy = pltpu.make_async_remote_copy(
        src_ref=source, dst_ref=target, send_sem=send_sem, recv_sem=recv_sem,
        device_id=device_id(place), device_id_type=MESH,
    )
    copy.start()
    return copy


def greet(grid, here):
    barrier = pltpu.get_barrier_semaphore()
    total = 0
    for dims in STAGES:
        for place in peers_of(grid, here, dims):
            pl.semaphore_signal(barrier, inc=1, device_id=device_id(place), device_id_type=MESH)
            total += 1
    return total


def sum_scratch(grid, tail, dtype):
    left, shapes = [0, 1, 2, 3], []
    for dims in STAGES:
        left = [dim for dim in left if dim not in dims]
        kept = tuple(grid[d] for d in left) + tail
        peers = peer_count(grid, dims)
        shapes += [
            pltpu.VMEM((peers,) + kept, dtype),
            pltpu.VMEM(kept, jnp.float32),
            pltpu.VMEM(kept if left else (16, 128), dtype),
            pltpu.SemaphoreType.DMA((peers,)),
            pltpu.SemaphoreType.DMA((peers,)),
        ]
    return shapes


class Scatter:
    def __init__(self, grid, here, own, sent, scratch):
        self.grid, self.here, self.own, self.sent = grid, here, own, sent
        self.scratch, self.left, self.stage = scratch, [0, 1, 2, 3], 0

    def block(self, place):
        dims = STAGES[self.stage]
        return tuple(place[d] if d in dims else slice(None) for d in self.left)

    def start(self):
        arrived, _, _, send, recv = self.scratch[5 * self.stage:5 * self.stage + 5]
        self.copies = [
            send_to(place, self.sent.at[self.block(place)], arrived.at[i], send.at[i], recv.at[i])
            for i, place in enumerate(peers_of(self.grid, self.here, STAGES[self.stage]))
        ]

    def finish(self):
        arrived, total, rounded, _, _ = self.scratch[5 * self.stage:5 * self.stage + 5]
        value = self.own[self.block(self.here)]
        for index, copy in enumerate(self.copies):
            copy.wait()
            value = value + arrived[index].astype(jnp.float32)
        total[...] = value
        self.own = total
        self.left = [dim for dim in self.left if dim not in STAGES[self.stage]]
        self.stage += 1
        if self.left:
            rounded[...] = value.astype(rounded.dtype)
            self.sent = rounded

    def advance(self):
        self.finish()
        if self.left:
            self.start()


class Counts:
    def __init__(self, grid, here, table, scratch):
        self.grid, self.here, self.table = grid, here, table
        self.scratch, self.stage = scratch, 0

    def start(self):
        arrived, _, send, recv = self.scratch[4 * self.stage:4 * self.stage + 4]
        self.copies = [
            send_to(place, self.table, arrived.at[i], send.at[i], recv.at[i])
            for i, place in enumerate(peers_of(self.grid, self.here, STAGES[self.stage]))
        ]

    def advance(self):
        arrived, total, _, _ = self.scratch[4 * self.stage:4 * self.stage + 4]
        value = self.table[...]
        for index, copy in enumerate(self.copies):
            copy.wait()
            value = value + arrived[index]
        total[...] = value
        self.table = total
        self.stage += 1
        if self.stage < len(STAGES):
            self.start()


def count_scratch(grid, tail):
    shapes = []
    for dims in STAGES:
        peers = peer_count(grid, dims)
        shapes += [
            pltpu.VMEM((peers,) + tail, jnp.float32),
            pltpu.VMEM(tail, jnp.float32),
            pltpu.SemaphoreType.DMA((peers,)),
            pltpu.SemaphoreType.DMA((peers,)),
        ]
    return shapes


class Gather:
    def __init__(self, grid, here, ref, sems):
        self.grid, self.here, self.ref, self.sems = grid, here, ref, sems

    def spread(self, block, places, sems):
        send, recv = sems
        return [
            send_to(place, block, block, send.at[i], recv.at[i]) for i, place in enumerate(places)
        ]

    def start(self):
        places = peers_of(self.grid, self.here, STAGES[2])
        self.copies = self.spread(self.ref.at[self.here], places, self.sems[0:2])

    def column(self, place):
        return self.ref.at[(slice(None),) + tuple(place[1:])]

    def forward(self, place):
        send, recv = self.sems[4:6]
        index = len(self.forwards)
        block = self.column(place)
        other = peers_of(self.grid, self.here, STAGES[0])[0]
        self.forwards.append(send_to(other, block, block, send.at[index], recv.at[index]))

    def second(self):
        for copy in self.copies:
            copy.wait()
        self.places = peers_of(self.grid, self.here, STAGES[1])
        self.copies = self.spread(self.column(self.here), self.places, self.sems[2:4])
        self.forwards = []
        self.forward(self.here)

    def third(self):
        for place, copy in reversed(list(zip(self.places, self.copies))):
            copy.wait()
            self.forward(place)

    def finish(self):
        for copy in self.forwards:
            copy.wait()


def gather_scratch(grid):
    counts = [peer_count(grid, STAGES[2]), peer_count(grid, STAGES[1]), peer_count(grid, STAGES[1]) + 1]
    return [pltpu.SemaphoreType.DMA((count,)) for count in counts for _ in range(2)]


class CopySpread:
    def __init__(self, grid, here, ref, sems):
        self.grid, self.here, self.ref, self.sems = grid, here, ref, sems

    def start(self):
        block = self.ref.at[self.here[R_HI], self.here[R_LO]]
        send, recv = self.sems[0:2]
        self.copies = [
            send_to(place, block, block, send.at[i], recv.at[i])
            for i, place in enumerate(peers_of(self.grid, self.here, (R_HI,)))
        ]

    def second(self):
        for copy in self.copies:
            copy.wait()
        block = self.ref.at[:, self.here[R_LO]]
        send, recv = self.sems[2:4]
        other = peers_of(self.grid, self.here, (R_LO,))[0]
        self.copies = [send_to(other, block, block, send.at[0], recv.at[0])]

    def finish(self):
        for copy in self.copies:
            copy.wait()


def layer_kernel(grid, kept, facts_hbm, owner_ref, slot_ref, feats_hbm, cot_hbm, w_hbm, w_upd_hbm,
                 ent_out_ref, fact_grad_hbm, left_out_ref, side_out_ref, *scratch):
    bf16, f32 = jnp.bfloat16, jnp.float32
    here = position()
    ent, rep = lax.axis_index("ent"), lax.axis_index("rep")
    n_rep = grid[R_HI] * grid[R_LO]
    greeted = greet(grid, here)
    scratch = list(scratch)

    def take(number):
        taken, scratch[:number] = scratch[:number], []
        return taken

    facts_ref, feats_ref, cot_ref, w_ref, w_upd_ref, in_sems, out_sems = take(7)
    pos_ref, gate_ref, d_pre_ref, spread_ref, hot_ref, hot_t, facts_t, w_t, w_upd_t = take(9)
    parts, parts_sent, all_refs = take(CHUNKS), take(CHUNKS), take(CHUNKS)
    count_ref, mean_ref, grad_z_ref = take(3)
    side_ref, side_sent, left_ref, left_sent = take(4)
    message_ref = d_pre_ref
    fact_rows, width = facts_ref.shape
    half = width // 2
    halves = [slice(0, half), slice(half, width)]
    every = (slice(None),) * 5
    piece = parts[0].shape[-2]
    share = piece * CHUNKS
    ent_rows = share * n_rep
    n_ents = ent_rows * grid[E_HI] * grid[E_LO]
    chunk = n_ents // CHUNKS
    block = fact_rows // 4
    rows_step = 4 * n_rep * piece

    counts = Counts(grid, here, count_ref, take(12))
    sums = [Scatter(grid, here, parts[c], parts_sent[c], take(15)) for c in range(CHUNKS)]
    spreads = [Gather(grid, here, all_refs[c], take(6)) for c in range(CHUNKS)]
    sides = Scatter(grid, here, side_ref, side_sent, take(15))
    lefts = [
        Scatter(grid, here, left_ref.at[every + (cols,)], left_sent.at[every + (cols,)], take(15))
        for cols in halves
    ]
    ent_spread = CopySpread(grid, here, ent_out_ref, take(4))

    def facts_copy(step):
        rows = pl.ds(pl.multiple_of(step * block, block), block)
        return pltpu.make_async_copy(facts_hbm.at[rows, :], facts_ref.at[rows, :], in_sems.at[step])

    others = [
        pltpu.make_async_copy(source, target, in_sems.at[4 + index])
        for index, (source, target) in enumerate([
            (w_hbm, w_ref), (w_upd_hbm, w_upd_ref), (cot_hbm, cot_ref), (feats_hbm, feats_ref)
        ])
    ]
    others[0].start()
    for step in range(4):
        facts_copy(step).start()
    for copy in others[1:]:
        copy.start()

    slot = slot_ref[...]
    pos_ref[...] = (
        lax.rem(slot, share) // piece * chunk
        + (owner_ref[...] * n_rep + slot // share) * piece
        + lax.rem(slot, piece)
    )
    others[0].wait()

    def project(step, carry):
        facts_copy(step).wait()
        rows = pl.ds(pl.multiple_of(step * block, block), block)
        pre = jnp.dot(facts_ref[rows, :], w_ref[...], preferred_element_type=f32)
        sig = jax.nn.sigmoid(pre)
        gate_ref[rows, :] = sig * (1.0 + pre * (1.0 - sig))
        message_ref[rows, :] = (pre * sig).astype(bf16)
        return carry

    lax.fori_loop(0, 4, project, 0)

    for c in range(CHUNKS):

        def gather_sums(step, carry, c=c):
            first = c * chunk + step * rows_step
            ids = lax.broadcasted_iota(jnp.int32, (rows_step, fact_rows), 0) + first
            hit = (ids == pos_ref[...]).astype(f32)
            hot = hit.astype(bf16)
            total = jnp.sum(hit, axis=1, keepdims=True)
            for low in range(rows_step // 128):
                column = jnp.broadcast_to(total[low * 128:(low + 1) * 128], (128, 128))
                count_ref[pl.ds(first // 128 + low, 1), :] = jnp.transpose(column)[0:1, :]
            agg = jnp.dot(hot, message_ref[...], preferred_element_type=f32)
            agg = agg.reshape(2, 2, grid[R_HI], 2, piece, width)
            parts[c][pl.ds(step * 2, 2)] = agg
            parts_sent[c][pl.ds(step * 2, 2)] = agg.astype(bf16)
            return carry

        lax.fori_loop(0, grid[E_HI] // 2, gather_sums, 0)
        if c == 0:
            pl.semaphore_wait(pltpu.get_barrier_semaphore(), greeted)
        sums[c].start()
    counts.start()

    def turn_facts(step, carry):
        rows = pl.ds(pl.multiple_of(step * block, block), block)
        facts_t[:, rows] = jnp.transpose(facts_ref[rows, :])
        return carry

    def hits_of(step, c):
        keys = jnp.concatenate([
            jnp.transpose(jnp.broadcast_to(
                pos_ref[:, pl.ds(pl.multiple_of(step * block + at, 128), 128)], (128, 128)
            ))
            for at in range(0, block, 128)
        ], axis=0)
        return jnp.concatenate([
            (keys == lax.broadcasted_iota(jnp.int32, (block, 128), 1) + (c * chunk + at))
            .astype(f32).astype(bf16)
            for at in range(0, chunk, 128)
        ], axis=1)

    def turn_hits(step, carry):
        rows = pl.ds(pl.multiple_of(step * block, block), block)
        for c in range(CHUNKS):
            hot_t[rows, c * chunk:(c + 1) * chunk] = hits_of(step, c)
        return carry

    def hits(step, c):
        if not kept:
            return hits_of(step, c)
        rows = pl.ds(pl.multiple_of(step * block, block), block)
        return hot_t[rows, c * chunk:(c + 1) * chunk]

    counts.advance()
    for item in sums:
        item.advance()
    for copy in others[1:]:
        copy.wait()
    w_upd_t[...] = jnp.transpose(w_upd_ref[...])
    w_t[...] = jnp.transpose(w_ref[...])
    lax.fori_loop(0, 4, turn_facts, 0)
    if kept:
        lax.fori_loop(0, 4, turn_hits, 0)
    counts.advance()
    for item in sums:
        item.advance()
    counts.advance()

    def entity(c):
        first = c * chunk + (ent * n_rep + rep) * piece
        table = counts.table[...]
        line = jnp.sum(
            jnp.where(
                lax.broadcasted_iota(jnp.int32, table.shape, 0) == first // 128, table, 0.0
            ), axis=0, keepdims=True,
        )
        lane = lax.broadcasted_iota(jnp.int32, (piece, 128), 1)
        row = lax.broadcasted_iota(jnp.int32, (piece, 128), 0) + lax.rem(first, 128)
        count = jnp.sum(
            jnp.where(lane == row, jnp.broadcast_to(line, (piece, 128)), 0.0),
            axis=1, keepdims=True,
        )
        denom = jnp.maximum(count, 1.0)
        rows = slice(c * piece, (c + 1) * piece)
        mean = (sums[c].own[...] / denom).astype(bf16)
        zval = jnp.dot(mean, w_upd_ref[...], preferred_element_type=f32)
        grad_z = (cot_ref[rep, rows].astype(f32) * silu_grad(zval)).astype(bf16)
        d_mean = jnp.dot(grad_z, w_upd_t[...], preferred_element_type=f32)
        all_refs[c][here] = (d_mean / denom).astype(bf16)
        spreads[c].start()
        mean_ref[rows, :] = mean
        grad_z_ref[rows, :] = grad_z
        value = feats_ref[rep, rows].astype(f32) + zval * jax.nn.sigmoid(zval)
        ent_out_ref[here[R_HI], here[R_LO], rows] = value.astype(bf16)

    for c in range(CHUNKS):
        sums[c].advance()
        entity(c)

    side = lax.dot_general(
        grad_z_ref[...], mean_ref[...], (((0,), (0,)), ((), ())), preferred_element_type=f32
    )
    side_ref[...] = side.reshape(side_ref.shape)
    side_sent[...] = side.astype(bf16).reshape(side_ref.shape)
    sides.start()
    for item in spreads:
        item.second()
    sides.finish()

    def expand_first(step, carry):
        rows = pl.ds(pl.multiple_of(step * block, block), block)
        spread_ref[rows, :] = jnp.dot(
            hits(step, 0), all_refs[0][...].reshape(chunk, width), preferred_element_type=f32
        )
        return carry

    spreads[0].third()
    spreads[0].finish()
    lax.fori_loop(0, 4, expand_first, 0)
    spreads[1].third()
    sides.start()
    ent_spread.start()
    spreads[1].finish()

    for number, cols in enumerate(halves):

        def expand(step, carry, cols=cols):
            rows = pl.ds(pl.multiple_of(step * block, block), block)
            table = all_refs[1][every + (cols,)].reshape(chunk, half)
            d_msg = spread_ref[rows, cols] + jnp.dot(
                hits(step, 1), table, preferred_element_type=f32
            )
            d_pre_ref[rows, cols] = (d_msg * gate_ref[rows, cols]).astype(bf16)
            return carry

        lax.fori_loop(0, 4, expand, 0)
        left = jnp.dot(facts_t[...], d_pre_ref[:, cols], preferred_element_type=f32)
        left = left.reshape(left_ref.shape[:-1] + (half,))
        left_ref[every + (cols,)] = left
        left_sent[every + (cols,)] = left.astype(bf16)
        lefts[number].start()
    sides.advance()
    ent_spread.second()
    for item in lefts:
        item.advance()

    grad_ref = facts_ref

    def grad_copy(step):
        rows = pl.ds(pl.multiple_of(step * block, block), block)
        return pltpu.make_async_copy(
            grad_ref.at[rows, :], fact_grad_hbm.at[rows, :], out_sems.at[step]
        )

    def fact_grads(step, carry):
        rows = pl.ds(pl.multiple_of(step * block, block), block)
        grad_ref[rows, :] = jnp.dot(
            d_pre_ref[rows, :], w_t[...], preferred_element_type=f32
        ).astype(bf16)
        grad_copy(step).start()
        return carry

    lax.fori_loop(0, 4, fact_grads, 0)
    sides.advance()
    side_out_ref[...] = sides.own[...]
    ent_spread.finish()
    for item in lefts:
        item.advance()
    for step in range(4):
        grad_copy(step).wait()
    for item in lefts:
        item.advance()
    left_out_ref[:, 0:half] = lefts[0].own[...]
    left_out_ref[:, half:width] = lefts[1].own[...]


def write_kernel(*refs):
    count = (len(refs) - 1) // 2
    sources, targets, sems = refs[:count], refs[count:2 * count], refs[-1]
    copies = []
    for source, target in zip(sources, targets):
        pieces = 4 if source.shape[0] % 64 == 0 and source.shape[0] > 1024 else 1
        rows = source.shape[0] // pieces
        for piece in range(pieces):
            at = pl.ds(piece * rows, rows)
            copies.append(
                pltpu.make_async_copy(source.at[at], target.at[at], sems.at[len(copies)])
            )
    for copy in copies:
        copy.start()
    for copy in copies:
        copy.wait()


def in_vmem(number):
    return [pl.BlockSpec(memory_space=pltpu.VMEM)] * number


def anywhere(number):
    return [pl.BlockSpec(memory_space=pl.ANY)] * number


def in_hbm(number):
    return [pl.BlockSpec(memory_space=pltpu.HBM)] * number


def per_device(facts, fact_owner, fact_slot, entity_feats, out_cotangent, w_msg, w_upd):
    n_owners = lax.axis_size("ent")
    n_copies = lax.axis_size("rep")
    grid = (n_owners // 2, 2, n_copies // 2, 2)
    fact_rows, width = facts.shape
    ent_rows = entity_feats.shape[0]
    ents = ent_rows * n_owners
    share = ent_rows // n_copies
    piece = share // CHUNKS
    bf16, f32 = jnp.bfloat16, jnp.float32
    rows = width // (n_owners * n_copies)
    half = width // 2
    kept = ents <= 1024
    table = (ents // 128, 128)
    ent_out, fact_grad, left, side = pl.pallas_call(
        functools.partial(layer_kernel, grid, kept),
        out_shape=(
            jax.ShapeDtypeStruct((grid[R_HI], grid[R_LO], share, width), bf16),
            jax.ShapeDtypeStruct((fact_rows, width), bf16),
            jax.ShapeDtypeStruct((rows, width), f32),
            jax.ShapeDtypeStruct((rows, width), f32),
        ),
        in_specs=in_hbm(1) + in_vmem(2) + in_hbm(4),
        out_specs=in_vmem(1) + anywhere(1) + in_vmem(2),
        scratch_shapes=(
            [
                pltpu.VMEM((fact_rows, width), bf16),
                pltpu.VMEM((n_copies, share, width), bf16),
                pltpu.VMEM((n_copies, share, width), bf16),
                pltpu.VMEM((width, width), bf16),
                pltpu.VMEM((width, width), bf16),
                pltpu.SemaphoreType.DMA((8,)),
                pltpu.SemaphoreType.DMA((4,)),
                pltpu.VMEM((1, fact_rows), jnp.int32),
                pltpu.VMEM((fact_rows, width), f32),
                pltpu.VMEM((fact_rows, width), bf16),
                pltpu.VMEM((fact_rows, width), f32),
                pltpu.VMEM((16, 128), bf16),
                pltpu.VMEM((fact_rows, ents) if kept else (16, 128), bf16),
                pltpu.VMEM((width, fact_rows), bf16),
                pltpu.VMEM((width, width), bf16),
                pltpu.VMEM((width, width), bf16),
            ]
            + [pltpu.VMEM(grid + (piece, width), f32)] * CHUNKS
            + [pltpu.VMEM(grid + (piece, width), bf16)] * (2 * CHUNKS)
            + [
                pltpu.VMEM(table, f32),
                pltpu.VMEM((share, width), bf16),
                pltpu.VMEM((share, width), bf16),
            ]
            + [
                pltpu.VMEM(grid + (rows, width), f32),
                pltpu.VMEM(grid + (rows, width), bf16),
            ] * 2
            + count_scratch(grid, table)
            + sum_scratch(grid, (piece, width), bf16) * CHUNKS
            + gather_scratch(grid) * CHUNKS
            + sum_scratch(grid, (rows, width), bf16)
            + sum_scratch(grid, (rows, half), bf16) * 2
            + [pltpu.SemaphoreType.DMA((grid[R_HI] - 1,))] * 2
            + [pltpu.SemaphoreType.DMA((1,))] * 2
        ),
        compiler_params=pltpu.CompilerParams(
            collective_id=0, has_side_effects=True, vmem_limit_bytes=(48 if kept else 60) << 20
        ),
    )(*[
        pltpu.with_memory_space_constraint(operand, pltpu.HBM)
        for operand in (
            facts,
            fact_owner.reshape(1, fact_rows),
            fact_slot.reshape(1, fact_rows),
            entity_feats.reshape(n_copies, share, width),
            out_cotangent.reshape(n_copies, share, width),
            w_msg,
            w_upd,
        )
    ])
    results = (ent_out.reshape(ent_rows, width), fact_grad, left, side)
    return pl.pallas_call(
        write_kernel,
        out_shape=tuple(jax.ShapeDtypeStruct(r.shape, r.dtype) for r in results),
        in_specs=anywhere(4),
        out_specs=in_hbm(4),
        scratch_shapes=[pltpu.SemaphoreType.DMA((8,))],
        compiler_params=pltpu.CompilerParams(vmem_limit_bytes=4 << 20),
    )(*results)


def solution(mesh):
    placed = (
        P(("ent", "rep"), None),
        P(("ent", "rep"), None),
        P(("ent", "rep")),
        P("ent", None),
        P("ent", None),
        P(),
        P(),
    )
    return jax.shard_map(
        per_device,
        mesh=mesh,
        in_specs=placed,
        out_specs=(
            P("ent", None),
            P(("ent", "rep"), None),
            P(("ent", "rep"), None),
            P(("ent", "rep"), None),
        ),
        check_vma=False,
    )
```

```python
import functools
import math

import jax
import jax.numpy as jnp
from jax import lax
from jax.experimental import pallas as pl
from jax.experimental.pallas import tpu as pltpu
from jax.sharding import PartitionSpec as P

E_HI, E_LO, R_HI, R_LO = range(4)
STAGES = ((R_LO,), (R_HI, E_LO), (E_HI,))
MESH = pl.DeviceIdType.MESH
CHUNKS = 2


def sigmoid(value):
    return 0.5 + 0.5 * jnp.tanh(0.5 * value)


def silu_grad(value):
    sig = sigmoid(value)
    return sig * (1.0 + value * (1.0 - sig))


def repeat(steps, body):
    if steps == 1:
        body(0, 0)
    else:
        lax.fori_loop(0, steps, body, 0)


def position():
    ent, rep = lax.axis_index("ent"), lax.axis_index("rep")
    return (ent // 2, lax.rem(ent, 2), rep // 2, lax.rem(rep, 2))


def peers_of(grid, here, dims):
    offsets = [()]
    for dim in dims:
        offsets = [offset + (step,) for offset in offsets for step in range(grid[dim])]
    offsets = sorted(offsets[1:], key=lambda offset: -sum(step > 0 for step in offset))
    places = []
    for offset in offsets:
        place = list(here)
        for dim, step in zip(dims, offset):
            place[dim] = lax.rem(here[dim] + step, grid[dim])
        places.append(tuple(place))
    return places


def peer_count(grid, dims):
    return math.prod(grid[dim] for dim in dims) - 1


def device_id(place):
    return {"ent": place[E_HI] * 2 + place[E_LO], "rep": place[R_HI] * 2 + place[R_LO]}


def send_to(place, source, target, send_sem, recv_sem):
    copy = pltpu.make_async_remote_copy(
        src_ref=source, dst_ref=target, send_sem=send_sem, recv_sem=recv_sem,
        device_id=device_id(place), device_id_type=MESH,
    )
    copy.start()
    return copy


def greet(grid, here):
    barrier = pltpu.get_barrier_semaphore()
    total = 0
    for dims in STAGES:
        for place in peers_of(grid, here, dims):
            pl.semaphore_signal(barrier, inc=1, device_id=device_id(place), device_id_type=MESH)
            total += 1
    return total


def sum_scratch(grid, tail, dtype):
    left, shapes = [0, 1, 2, 3], []
    for dims in STAGES:
        left = [dim for dim in left if dim not in dims]
        kept = tuple(grid[d] for d in left) + tail
        peers = peer_count(grid, dims)
        shapes += [
            pltpu.VMEM((peers,) + kept, dtype),
            pltpu.VMEM(kept, jnp.float32),
            pltpu.VMEM(kept if left else (16, 128), dtype),
            pltpu.SemaphoreType.DMA((peers,)),
            pltpu.SemaphoreType.DMA((peers,)),
        ]
    return shapes


class Scatter:
    def __init__(self, grid, here, own, sent, scratch, stage=0):
        self.grid, self.here, self.own, self.sent = grid, here, own, sent
        self.scratch, self.stage = [None] * (5 * stage) + scratch, stage
        self.left = [d for d in range(4) if all(d not in dims for dims in STAGES[:stage])]

    def block(self, place):
        dims = STAGES[self.stage]
        return tuple(place[d] if d in dims else slice(None) for d in self.left)

    def start(self):
        arrived, _, _, send, recv = self.scratch[5 * self.stage:5 * self.stage + 5]
        self.copies = [
            send_to(place, self.sent.at[self.block(place)], arrived.at[i], send.at[i], recv.at[i])
            for i, place in enumerate(peers_of(self.grid, self.here, STAGES[self.stage]))
        ]

    def finish(self):
        arrived, total, rounded, _, _ = self.scratch[5 * self.stage:5 * self.stage + 5]
        value = self.own[self.block(self.here)]
        for index, copy in enumerate(self.copies):
            copy.wait()
            value = value + arrived[index].astype(jnp.float32)
        total[...] = value
        self.own = total
        self.left = [dim for dim in self.left if dim not in STAGES[self.stage]]
        self.stage += 1
        if self.left:
            rounded[...] = value.astype(rounded.dtype)
            self.sent = rounded

    def advance(self):
        self.finish()
        if self.left:
            self.start()


class Counts:
    def __init__(self, grid, here, table, scratch):
        self.grid, self.here, self.table = grid, here, table
        self.scratch, self.stage = scratch, 0

    def start(self):
        arrived, _, send, recv = self.scratch[4 * self.stage:4 * self.stage + 4]
        self.copies = [
            send_to(place, self.table, arrived.at[i], send.at[i], recv.at[i])
            for i, place in enumerate(peers_of(self.grid, self.here, STAGES[self.stage]))
        ]

    def advance(self):
        arrived, total, _, _ = self.scratch[4 * self.stage:4 * self.stage + 4]
        value = self.table[...]
        for index, copy in enumerate(self.copies):
            copy.wait()
            value = value + arrived[index]
        total[...] = value
        self.table = total
        self.stage += 1
        if self.stage < len(STAGES):
            self.start()


def count_scratch(grid, tail):
    shapes = []
    for dims in STAGES:
        peers = peer_count(grid, dims)
        shapes += [
            pltpu.VMEM((peers,) + tail, jnp.float32),
            pltpu.VMEM(tail, jnp.float32),
            pltpu.SemaphoreType.DMA((peers,)),
            pltpu.SemaphoreType.DMA((peers,)),
        ]
    return shapes


class Gather:
    def __init__(self, grid, here, ref, sems):
        self.grid, self.here, self.ref, self.sems = grid, here, ref, sems

    def spread(self, block, places, sems):
        send, recv = sems
        return [
            send_to(place, block, block, send.at[i], recv.at[i]) for i, place in enumerate(places)
        ]

    def start(self):
        places = peers_of(self.grid, self.here, STAGES[2])
        self.copies = self.spread(self.ref.at[self.here], places, self.sems[0:2])

    def column(self, place):
        return self.ref.at[(slice(None),) + tuple(place[1:])]

    def forward(self, place):
        send, recv = self.sems[4:6]
        index = len(self.forwards)
        block = self.column(place)
        other = peers_of(self.grid, self.here, STAGES[0])[0]
        self.forwards.append(send_to(other, block, block, send.at[index], recv.at[index]))

    def second(self):
        for copy in self.copies:
            copy.wait()
        self.places = peers_of(self.grid, self.here, STAGES[1])
        self.copies = self.spread(self.column(self.here), self.places, self.sems[2:4])
        self.forwards = []
        self.forward(self.here)

    def third(self):
        for place, copy in reversed(list(zip(self.places, self.copies))):
            copy.wait()
            self.forward(place)

    def finish(self):
        for copy in self.forwards:
            copy.wait()


def gather_scratch(grid):
    counts = [peer_count(grid, STAGES[2]), peer_count(grid, STAGES[1]), peer_count(grid, STAGES[1]) + 1]
    return [pltpu.SemaphoreType.DMA((count,)) for count in counts for _ in range(2)]


def layer_kernel(grid, kept, facts_hbm, owner_hbm, slot_hbm, feats_hbm, cot_hbm, w_hbm, w_upd_hbm,
                 ent_out_ref, fact_grad_hbm, left_out_ref, side_out_ref, *scratch):
    bf16, f32 = jnp.bfloat16, jnp.float32
    here = position()
    ent, rep = lax.axis_index("ent"), lax.axis_index("rep")
    n_rep = grid[R_HI] * grid[R_LO]
    greeted = greet(grid, here)
    scratch = list(scratch)

    def take(number):
        taken, scratch[:number] = scratch[:number], []
        return taken

    facts_ref, feats_ref, cot_ref, w_ref, w_upd_ref, in_sems, out_sems = take(7)
    owner_ref, slot_ref = take(2)
    pos_ref, gate_ref, d_pre_ref, spread_ref, hot_ref, hot_t, facts_t, w_t, w_upd_t = take(9)
    parts, parts_sent, all_refs = take(CHUNKS), take(CHUNKS), take(CHUNKS)
    count_ref, pair_ref, pair_send, pair_recv, core_send, core_recv = take(6)
    side_ref, side_sent, left_ref, left_sent = take(4)
    message_ref = d_pre_ref
    fact_rows, width = facts_ref.shape
    half = width // 2
    halves = [slice(0, half), slice(half, width)]
    every = (slice(None),) * 5
    piece = parts[0].shape[-2]
    share = piece * CHUNKS
    ent_rows = share * n_rep
    n_ents = ent_rows * grid[E_HI] * grid[E_LO]
    chunk = n_ents // CHUNKS
    block = fact_rows // 4
    tall = 4 if grid[E_HI] % 4 == 0 else 2
    rows_step = tall * 2 * n_rep * piece
    sum_steps = grid[E_HI] // tall
    expand_steps = 1 if kept else 4
    expand_block = fact_rows // expand_steps

    counts = Counts(grid, here, count_ref, take(12))
    sums = [Scatter(grid, here, parts[c], parts_sent[c], take(15)) for c in range(CHUNKS)]
    spreads = [Gather(grid, here, all_refs[c], take(6)) for c in range(CHUNKS)]
    own_rows = (slice(None),) + here[1:]
    sides = Scatter(grid, here, side_ref.at[own_rows], side_sent, take(5), stage=2)
    lefts = [
        Scatter(grid, here, left_ref.at[every + (cols,)], left_sent.at[every + (cols,)], take(15))
        for cols in halves
    ]

    def facts_copy(step):
        rows = pl.ds(pl.multiple_of(step * block, block), block)
        return pltpu.make_async_copy(facts_hbm.at[rows, :], facts_ref.at[rows, :], in_sems.at[step])

    others = [
        pltpu.make_async_copy(source, target, in_sems.at[4 + index])
        for index, (source, target) in enumerate([
            (owner_hbm, owner_ref), (slot_hbm, slot_ref), (w_hbm, w_ref),
            (w_upd_hbm, w_upd_ref), (cot_hbm, cot_ref), (feats_hbm, feats_ref),
        ])
    ]
    for copy in others[:3]:
        copy.start()
    for step in range(4):
        facts_copy(step).start()
    for copy in others[:2]:
        copy.wait()
    slot = slot_ref[...]
    pos_ref[...] = (
        lax.rem(slot, share) // piece * chunk
        + (owner_ref[...] * n_rep + slot // share) * piece
        + lax.rem(slot, piece)
    )

    def one_hot(rows, first, entries):
        ids = lax.broadcasted_iota(jnp.int32, (rows, fact_rows), 0) + first
        return (ids == entries).astype(f32).astype(bf16)

    def find_hits(first):
        return one_hot(rows_step, first, pos_ref[...])

    lines = count_ref.shape[0]
    table = lax.dot_general(
        one_hot(max(lines, 16), 0, pos_ref[...] // 128),
        one_hot(128, 0, lax.rem(pos_ref[...], 128)),
        (((1,), (1,)), ((), ())), preferred_element_type=f32,
    )
    count_ref[...] = table[0:lines]

    def hot_rows(first):
        if sum_steps == 1:
            return slice(first, first + rows_step)
        return pl.ds(pl.multiple_of(first, rows_step), rows_step)

    def prepare(step, carry):
        hot_ref[hot_rows(step * rows_step), :] = find_hits(step * rows_step)
        return carry

    if kept:
        repeat(sum_steps, prepare)
    others[2].wait()

    def project(first, count):
        for index in range(first, first + count):
            facts_copy(index).wait()
        rows = slice(first * block, (first + count) * block)
        half_pre = 0.5 * jnp.dot(facts_ref[rows, :], w_ref[...], preferred_element_type=f32)
        message_ref[rows, :] = (half_pre + half_pre * jnp.tanh(half_pre)).astype(bf16)

    for first, count in ((0, 2), (2, 2)):
        project(first, count)
    for copy in others[3:]:
        copy.start()

    for c in range(CHUNKS):

        def gather_sums(step, carry, c=c):
            first = c * chunk + step * rows_step
            hot = hot_ref[hot_rows(first), :] if kept else find_hits(first)
            agg = jnp.dot(hot, message_ref[...], preferred_element_type=f32)
            if kept and c + 1 < CHUNKS:
                hot_ref[hot_rows(first + chunk), :] = find_hits(first + chunk)
            agg = agg.reshape(tall, 2, grid[R_HI], 2, piece, width)
            parts[c][pl.ds(step * tall, tall)] = agg
            parts_sent[c][pl.ds(step * tall, tall)] = agg.astype(bf16)
            return carry

        repeat(sum_steps, gather_sums)
        if c == 0:
            pl.semaphore_wait(pltpu.get_barrier_semaphore(), greeted)
        sums[c].start()
        if c == 0:
            counts.start()

    def turn_facts(step, carry):
        rows = pl.ds(pl.multiple_of(step * block, block), block)
        facts_t[:, rows] = jnp.transpose(facts_ref[rows, :])
        return carry

    def open_gate(step, carry):
        rows = pl.ds(pl.multiple_of(step * 2 * block, 2 * block), 2 * block)
        pre = jnp.dot(facts_ref[rows, :], w_ref[...], preferred_element_type=f32)
        gate_ref[rows, :] = silu_grad(pre)
        return carry

    def hits_of(step, c):
        keys = jnp.concatenate([
            jnp.transpose(jnp.broadcast_to(
                pos_ref[:, pl.ds(pl.multiple_of(step * block + at, 128), 128)], (128, 128)
            ))
            for at in range(0, block, 128)
        ], axis=0)
        return jnp.concatenate([
            (keys == lax.broadcasted_iota(jnp.int32, (block, 128), 1) + (c * chunk + at))
            .astype(f32).astype(bf16)
            for at in range(0, chunk, 128)
        ], axis=1)

    def turn_hits(step, carry):
        rows = pl.ds(pl.multiple_of(step * block, block), block)
        for c in range(CHUNKS):
            hot_t[rows, c * chunk:(c + 1) * chunk] = hits_of(step, c)
        return carry

    def hits(step, c):
        if not kept:
            return hits_of(step, c)
        return hot_t[:, c * chunk:(c + 1) * chunk]

    def expand_rows(step):
        if expand_steps == 1:
            return slice(0, fact_rows)
        return pl.ds(pl.multiple_of(step * expand_block, expand_block), expand_block)

    sums[0].advance()
    counts.advance()
    sums[1].advance()
    for copy in others[3:]:
        copy.wait()
    w_upd_t[...] = jnp.transpose(w_upd_ref[...])
    w_t[...] = jnp.transpose(w_ref[...])
    lax.fori_loop(0, 4, turn_facts, 0)
    if kept:
        lax.fori_loop(0, 4, turn_hits, 0)
    sums[0].advance()
    counts.advance()
    sums[1].advance()
    lax.fori_loop(0, 2, open_gate, 0)

    def entity(c):
        first = c * chunk + (ent * n_rep + rep) * piece
        table = counts.table[...]
        line = jnp.sum(
            jnp.where(
                lax.broadcasted_iota(jnp.int32, table.shape, 0) == first // 128, table, 0.0
            ), axis=0, keepdims=True,
        )
        lane = lax.broadcasted_iota(jnp.int32, (piece, 128), 1)
        row = lax.broadcasted_iota(jnp.int32, (piece, 128), 0) + lax.rem(first, 128)
        count = jnp.sum(
            jnp.where(lane == row, jnp.broadcast_to(line, (piece, 128)), 0.0),
            axis=1, keepdims=True,
        )
        denom = jnp.maximum(count, 1.0)
        rows = slice(c * piece, (c + 1) * piece)
        mean = (sums[c].own[...] / denom).astype(bf16)
        zval = jnp.dot(mean, w_upd_ref[...], preferred_element_type=f32)
        grad_z = (cot_ref[rep, rows].astype(f32) * silu_grad(zval)).astype(bf16)
        d_mean = jnp.dot(grad_z, w_upd_t[...], preferred_element_type=f32)
        all_refs[c][here] = (d_mean / denom).astype(bf16)
        spreads[c].start()
        pair = pair_ref.at[here[1:] + (c,)]
        pair[:, 0:width] = mean
        pair[:, width:2 * width] = grad_z
        for place in group:
            index = len(pair_copies)
            pair_copies.append(
                send_to(place, pair, pair, pair_send.at[index], pair_recv.at[index])
            )

    group = peers_of(grid, here, STAGES[1])
    pair_copies = []
    counts.advance()
    for c in range(CHUNKS):
        sums[c].finish()
        entity(c)
    for item in spreads:
        item.second()
    for copy in pair_copies:
        copy.wait()
    pairs = pair_ref.at[:, :, here[R_LO]]
    other = peers_of(grid, here, STAGES[0])[0]
    pair_copy = send_to(other, pairs, pairs, core_send.at[0], core_recv.at[0])

    def expand_first(step, carry):
        spread_ref[expand_rows(step), :] = jnp.dot(
            hits(step, 0), all_refs[0][...].reshape(chunk, width), preferred_element_type=f32
        ).astype(bf16)
        return carry

    spreads[0].third()
    spreads[0].finish()
    repeat(expand_steps, expand_first)
    spreads[1].third()
    spreads[1].finish()

    for number, cols in enumerate(halves):

        def expand(step, carry, cols=cols):
            rows = expand_rows(step)
            table = all_refs[1][every + (cols,)].reshape(chunk, half)
            d_msg = spread_ref[rows, cols].astype(f32) + jnp.dot(
                hits(step, 1), table, preferred_element_type=f32
            )
            d_pre_ref[rows, cols] = (d_msg * gate_ref[rows, cols]).astype(bf16)
            return carry

        repeat(expand_steps, expand)
        left = jnp.dot(facts_t[...], d_pre_ref[:, cols], preferred_element_type=f32)
        left = left.reshape(left_ref.shape[:-1] + (half,))
        left_ref[every + (cols,)] = left
        left_sent[every + (cols,)] = left.astype(bf16)
        lefts[number].start()
    lefts[0].advance()
    pair_copy.wait()
    pair = pair_ref[...].reshape(2 * grid[R_HI] * 2 * share, 2 * width)
    side = lax.dot_general(
        pair[:, width:2 * width], pair[:, 0:width],
        (((0,), (0,)), ((), ())), preferred_element_type=f32,
    )
    side_ref[...] = side.reshape(side_ref.shape)
    side_sent[...] = side_ref[own_rows].astype(bf16)
    sides.start()
    lefts[1].advance()
    means = pair_ref[here[E_LO], :, :, :, :, 0:width].reshape(ent_rows, width)
    zval = jnp.dot(means, w_upd_ref[...], preferred_element_type=f32)
    feats = feats_ref[...].reshape(ent_rows, width).astype(f32)
    ent_out_ref[...] = (feats + zval * sigmoid(zval)).astype(bf16)

    grad_ref = facts_ref

    def grad_copy(step):
        rows = pl.ds(pl.multiple_of(step * block, block), block)
        return pltpu.make_async_copy(
            grad_ref.at[rows, :], fact_grad_hbm.at[rows, :], out_sems.at[step]
        )

    def fact_grads(step, carry):
        rows = pl.ds(pl.multiple_of(step * block, block), block)
        grad_ref[rows, :] = jnp.dot(
            d_pre_ref[rows, :], w_t[...], preferred_element_type=f32
        ).astype(bf16)
        grad_copy(step).start()
        return carry

    lax.fori_loop(0, 4, fact_grads, 0)
    for item in lefts:
        item.advance()
    sides.finish()
    side_out_ref[...] = sides.own[...]
    for step in range(4):
        grad_copy(step).wait()
    for item in lefts:
        item.advance()
    left_out_ref[:, 0:half] = lefts[0].own[...]
    left_out_ref[:, half:width] = lefts[1].own[...]


def write_kernel(*refs):
    count = (len(refs) - 1) // 2
    sources, targets, sems = refs[:count], refs[count:2 * count], refs[-1]
    copies = []
    for source, target in zip(sources, targets):
        pieces = 4 if source.shape[0] % 64 == 0 and source.shape[0] > 1024 else 1
        rows = source.shape[0] // pieces
        for piece in range(pieces):
            at = pl.ds(piece * rows, rows)
            copies.append(
                pltpu.make_async_copy(source.at[at], target.at[at], sems.at[len(copies)])
            )
    for copy in copies:
        copy.start()
    for copy in copies:
        copy.wait()


def in_vmem(number):
    return [pl.BlockSpec(memory_space=pltpu.VMEM)] * number


def anywhere(number):
    return [pl.BlockSpec(memory_space=pl.ANY)] * number


def in_hbm(number):
    return [pl.BlockSpec(memory_space=pltpu.HBM)] * number


def per_device(facts, fact_owner, fact_slot, entity_feats, out_cotangent, w_msg, w_upd):
    n_owners = lax.axis_size("ent")
    n_copies = lax.axis_size("rep")
    grid = (n_owners // 2, 2, n_copies // 2, 2)
    fact_rows, width = facts.shape
    ent_rows = entity_feats.shape[0]
    ents = ent_rows * n_owners
    share = ent_rows // n_copies
    piece = share // CHUNKS
    bf16, f32 = jnp.bfloat16, jnp.float32
    rows = width // (n_owners * n_copies)
    half = width // 2
    kept = ents <= 1024
    table = (ents // 128, 128)
    ent_out, fact_grad, left, side = pl.pallas_call(
        functools.partial(layer_kernel, grid, kept),
        out_shape=(
            jax.ShapeDtypeStruct((ent_rows, width), bf16),
            jax.ShapeDtypeStruct((fact_rows, width), bf16),
            jax.ShapeDtypeStruct((rows, width), f32),
            jax.ShapeDtypeStruct((rows, width), f32),
        ),
        in_specs=in_hbm(7),
        out_specs=in_vmem(1) + anywhere(1) + in_vmem(2),
        scratch_shapes=(
            [
                pltpu.VMEM((fact_rows, width), bf16),
                pltpu.VMEM((n_copies, share, width), bf16),
                pltpu.VMEM((n_copies, share, width), bf16),
                pltpu.VMEM((width, width), bf16),
                pltpu.VMEM((width, width), bf16),
                pltpu.SemaphoreType.DMA((10,)),
                pltpu.SemaphoreType.DMA((4,)),
                pltpu.VMEM((1, fact_rows), jnp.int32),
                pltpu.VMEM((1, fact_rows), jnp.int32),
                pltpu.VMEM((1, fact_rows), jnp.int32),
                pltpu.VMEM((fact_rows, width), f32),
                pltpu.VMEM((fact_rows, width), bf16),
                pltpu.VMEM((fact_rows, width), bf16),
                pltpu.VMEM((ents, fact_rows) if kept else (16, 128), bf16),
                pltpu.VMEM((fact_rows, ents) if kept else (16, 128), bf16),
                pltpu.VMEM((width, fact_rows), bf16),
                pltpu.VMEM((width, width), bf16),
                pltpu.VMEM((width, width), bf16),
            ]
            + [pltpu.VMEM(grid + (piece, width), f32)] * CHUNKS
            + [pltpu.VMEM(grid + (piece, width), bf16)] * (2 * CHUNKS)
            + [
                pltpu.VMEM(table, f32),
                pltpu.VMEM(grid[1:] + (CHUNKS, piece, 2 * width), bf16),
                pltpu.SemaphoreType.DMA((CHUNKS * peer_count(grid, STAGES[1]),)),
                pltpu.SemaphoreType.DMA((CHUNKS * peer_count(grid, STAGES[1]),)),
                pltpu.SemaphoreType.DMA((1,)),
                pltpu.SemaphoreType.DMA((1,)),
            ]
            + [
                pltpu.VMEM(grid + (rows, width), f32),
                pltpu.VMEM((grid[E_HI], rows, width), bf16),
                pltpu.VMEM(grid + (rows, width), f32),
                pltpu.VMEM(grid + (rows, width), bf16),
            ]
            + count_scratch(grid, table)
            + sum_scratch(grid, (piece, width), bf16) * CHUNKS
            + gather_scratch(grid) * CHUNKS
            + sum_scratch(grid, (rows, width), bf16)[10:]
            + sum_scratch(grid, (rows, half), bf16) * 2
        ),
        compiler_params=pltpu.CompilerParams(
            collective_id=0, has_side_effects=True, vmem_limit_bytes=(48 if kept else 60) << 20
        ),
    )(*[
        pltpu.with_memory_space_constraint(operand, pltpu.HBM)
        for operand in (
            facts,
            fact_owner.reshape(1, fact_rows),
            fact_slot.reshape(1, fact_rows),
            entity_feats.reshape(n_copies, share, width),
            out_cotangent.reshape(n_copies, share, width),
            w_msg,
            w_upd,
        )
    ])
    results = (ent_out, fact_grad, left, side)
    return pl.pallas_call(
        write_kernel,
        out_shape=tuple(jax.ShapeDtypeStruct(r.shape, r.dtype) for r in results),
        in_specs=anywhere(4),
        out_specs=in_hbm(4),
        scratch_shapes=[pltpu.SemaphoreType.DMA((8,))],
        compiler_params=pltpu.CompilerParams(vmem_limit_bytes=4 << 20),
    )(*results)


def solution(mesh):
    placed = (
        P(("ent", "rep"), None),
        P(("ent", "rep"), None),
        P(("ent", "rep")),
        P("ent", None),
        P("ent", None),
        P(),
        P(),
    )
    return jax.shard_map(
        per_device,
        mesh=mesh,
        in_specs=placed,
        out_specs=(
            P("ent", None),
            P(("ent", "rep"), None),
            P(("ent", "rep"), None),
            P(("ent", "rep"), None),
        ),
        check_vma=False,
    )
```

```python
import functools
import math

import jax
import jax.numpy as jnp
from jax import lax
from jax.experimental import pallas as pl
from jax.experimental.pallas import tpu as pltpu
from jax.sharding import PartitionSpec as P

E_HI, E_LO, R_HI, R_LO = range(4)
STAGES = ((R_LO,), (R_HI, E_LO), (E_HI,))
ALL = (E_HI, E_LO, R_HI, R_LO)
MESH = pl.DeviceIdType.MESH
CHUNKS = 2


def sigmoid(value):
    return 0.5 + 0.5 * jnp.tanh(0.5 * value)


def silu_grad(value):
    sig = sigmoid(value)
    return sig * (1.0 + value * (1.0 - sig))


def cut_of(width):
    return 3 * width // 4 // 128 * 128


def repeat(steps, body):
    if steps == 1:
        body(0, 0)
    else:
        lax.fori_loop(0, steps, body, 0)


def position():
    ent, rep = lax.axis_index("ent"), lax.axis_index("rep")
    return (ent // 2, lax.rem(ent, 2), rep // 2, lax.rem(rep, 2))


def peers_of(grid, here, dims, sources=False):
    offsets = [()]
    for dim in dims:
        offsets = [offset + (step,) for offset in offsets for step in range(grid[dim])]
    offsets = sorted(offsets[1:], key=lambda offset: -sum(step > 0 for step in offset))
    places = []
    for offset in offsets:
        place = list(here)
        for dim, step in zip(dims, offset):
            ahead = grid[dim] - step if sources and step else step
            place[dim] = lax.rem(here[dim] + ahead, grid[dim])
        places.append(tuple(place))
    return places


def peer_count(grid, dims):
    return math.prod(grid[dim] for dim in dims) - 1


def device_id(place):
    return {"ent": place[E_HI] * 2 + place[E_LO], "rep": place[R_HI] * 2 + place[R_LO]}


def send_to(place, source, target, send_sem, recv_sem):
    copy = pltpu.make_async_remote_copy(
        src_ref=source, dst_ref=target, send_sem=send_sem, recv_sem=recv_sem,
        device_id=device_id(place), device_id_type=MESH,
    )
    copy.start()
    return copy


def greet(grid, here):
    barrier = pltpu.get_barrier_semaphore()
    total = 0
    for dims in STAGES:
        for place in peers_of(grid, here, dims):
            pl.semaphore_signal(barrier, inc=1, device_id=device_id(place), device_id_type=MESH)
            total += 1
    return total


def sum_scratch(grid, tail, dtype, stages=STAGES, left=ALL):
    shapes = []
    for dims in stages:
        left = [dim for dim in left if dim not in dims]
        kept = tuple(grid[d] for d in left) + tail
        peers = peer_count(grid, dims)
        shapes += [
            pltpu.VMEM((peers,) + kept, dtype),
            pltpu.VMEM(kept, jnp.float32),
            pltpu.VMEM(kept if left else (16, 128), dtype),
            pltpu.SemaphoreType.DMA((peers,)),
            pltpu.SemaphoreType.DMA((peers,)),
        ]
    return shapes


class Scatter:
    def __init__(self, grid, here, own, sent, scratch, stages=STAGES, left=ALL):
        self.grid, self.here, self.own, self.sent = grid, here, own, sent
        self.scratch, self.stages, self.left, self.stage = scratch, stages, left, 0

    def block(self, place):
        dims = self.stages[self.stage]
        return tuple(place[d] if d in dims else slice(None) for d in self.left)

    def start(self):
        arrived, _, _, send, recv = self.scratch[5 * self.stage:5 * self.stage + 5]
        self.copies = [
            send_to(place, self.sent.at[self.block(place)], arrived.at[i], send.at[i], recv.at[i])
            for i, place in enumerate(peers_of(self.grid, self.here, self.stages[self.stage]))
        ]

    def finish(self):
        arrived, total, rounded, _, _ = self.scratch[5 * self.stage:5 * self.stage + 5]
        value = self.own[self.block(self.here)]
        for index, copy in enumerate(self.copies):
            copy.wait()
            value = value + arrived[index].astype(jnp.float32)
        total[...] = value
        self.own = total
        self.left = [dim for dim in self.left if dim not in self.stages[self.stage]]
        self.stage += 1
        if self.left:
            rounded[...] = value.astype(rounded.dtype)
            self.sent = rounded

    def advance(self):
        self.finish()
        if self.left:
            self.start()


class SplitScatter:
    def __init__(self, grid, here, own, sent, scratch, cut):
        self.grid, self.here, self.scratch, self.cut = grid, here, scratch[5:], cut
        self.first = Scatter(grid, here, own, sent, scratch[:5], STAGES[:1])
        self.start = self.first.start

    def split(self):
        self.first.finish()
        self.parts = []
        for index, (cols, stages) in enumerate([
            (slice(0, self.cut), (STAGES[1], STAGES[2])),
            (slice(self.cut, None), (STAGES[2], STAGES[1])),
        ]):
            view = (slice(None),) * (len(self.first.left) + 1)
            width = self.first.own.shape[-1]
            view += (slice(cols.start, cols.stop or width),)
            self.parts.append(Scatter(
                self.grid, self.here, self.first.own.at[view], self.first.sent.at[view],
                self.scratch[10 * index:10 * index + 10], stages, self.first.left,
            ))
        for part in self.parts:
            part.start()

    def advance(self):
        for part in reversed(self.parts):
            part.advance()

    def finish(self):
        for part in reversed(self.parts):
            part.finish()

    def value(self):
        return jnp.concatenate([part.own[...] for part in self.parts], axis=1)


def split_scratch(grid, rows, width, cut, dtype):
    return (
        sum_scratch(grid, (rows, width), dtype, STAGES[:1])
        + sum_scratch(grid, (rows, cut), dtype, (STAGES[1], STAGES[2]), ALL[:3])
        + sum_scratch(grid, (rows, width - cut), dtype, (STAGES[2], STAGES[1]), ALL[:3])
    )


class Counts:
    def __init__(self, grid, here, table, scratch):
        self.grid, self.here, self.table = grid, here, table
        self.scratch, self.stage = scratch, 0

    def start(self):
        arrived, _, send, recv = self.scratch[4 * self.stage:4 * self.stage + 4]
        self.copies = [
            send_to(place, self.table, arrived.at[i], send.at[i], recv.at[i])
            for i, place in enumerate(peers_of(self.grid, self.here, STAGES[self.stage]))
        ]

    def advance(self):
        arrived, total, _, _ = self.scratch[4 * self.stage:4 * self.stage + 4]
        value = self.table[...]
        for index, copy in enumerate(self.copies):
            copy.wait()
            value = value + arrived[index]
        total[...] = value
        self.table = total
        self.stage += 1
        if self.stage < len(STAGES):
            self.start()


def count_scratch(grid, tail):
    shapes = []
    for dims in STAGES:
        peers = peer_count(grid, dims)
        shapes += [
            pltpu.VMEM((peers,) + tail, jnp.float32),
            pltpu.VMEM(tail, jnp.float32),
            pltpu.SemaphoreType.DMA((peers,)),
            pltpu.SemaphoreType.DMA((peers,)),
        ]
    return shapes


class Gather:
    def __init__(self, grid, here, ref, sems, order, cols):
        self.grid, self.here, self.ref, self.sems = grid, here, ref, sems
        self.order, self.cols = order, cols

    def spread(self, block, dims, sems):
        send, recv = sems
        self.places = peers_of(self.grid, self.here, dims, sources=True)
        self.copies = [
            send_to(place, block, block, send.at[i], recv.at[i])
            for i, place in enumerate(peers_of(self.grid, self.here, dims))
        ]

    def block(self, place, held):
        index = tuple(slice(None) if d in held else place[d] for d in ALL)
        return self.ref.at[index + (slice(None), self.cols)]

    def start(self):
        self.spread(self.block(self.here, ()), self.order[0], self.sems[0:2])

    def forward(self, place):
        send, recv = self.sems[4:6]
        index = len(self.forwards)
        block = self.block(place, self.order[0])
        other = peers_of(self.grid, self.here, STAGES[0])[0]
        self.forwards.append(send_to(other, block, block, send.at[index], recv.at[index]))

    def second(self):
        for copy in self.copies:
            copy.wait()
        self.spread(self.block(self.here, self.order[0]), self.order[1], self.sems[2:4])
        self.forwards = []
        self.forward(self.here)

    def third(self):
        for place, copy in reversed(list(zip(self.places, self.copies))):
            copy.wait()
            self.forward(place)

    def finish(self):
        for copy in self.forwards:
            copy.wait()


def gather_scratch(grid, order):
    counts = [peer_count(grid, order[0]), peer_count(grid, order[1]), peer_count(grid, order[1]) + 1]
    return [pltpu.SemaphoreType.DMA((count,)) for count in counts for _ in range(2)]


def layer_kernel(grid, kept, facts_hbm, owner_hbm, slot_hbm, feats_hbm, cot_hbm, w_hbm, w_upd_hbm,
                 ent_out_ref, fact_grad_hbm, left_out_ref, side_out_ref, *scratch):
    bf16, f32 = jnp.bfloat16, jnp.float32
    here = position()
    ent, rep = lax.axis_index("ent"), lax.axis_index("rep")
    n_rep = grid[R_HI] * grid[R_LO]
    greeted = greet(grid, here)
    scratch = list(scratch)

    def take(number):
        taken, scratch[:number] = scratch[:number], []
        return taken

    facts_ref, feats_ref, cot_ref, w_ref, w_upd_ref, in_sems, out_sems = take(7)
    owner_ref, slot_ref = take(2)
    pos_ref, gate_ref, d_pre_ref, spread_ref, hot_ref, hot_t, facts_t, w_t, w_upd_t = take(9)
    parts, parts_sent, all_refs = take(CHUNKS), take(CHUNKS), take(CHUNKS)
    count_ref, pair_ref, pair_send, pair_recv, core_send, core_recv = take(6)
    side_ref, side_sent, left_ref, left_sent = take(4)
    message_ref = d_pre_ref
    fact_rows, width = facts_ref.shape
    half = width // 2
    halves = [slice(0, half), slice(half, width)]
    every = (slice(None),) * 5
    piece = parts[0].shape[-2]
    share = piece * CHUNKS
    ent_rows = share * n_rep
    n_ents = ent_rows * grid[E_HI] * grid[E_LO]
    chunk = n_ents // CHUNKS
    block = fact_rows // 4
    tall = 4 if grid[E_HI] % 4 == 0 else 2
    rows_step = tall * 2 * n_rep * piece
    sum_steps = grid[E_HI] // tall
    expand_steps = 1 if kept else 4
    expand_block = fact_rows // expand_steps

    counts = Counts(grid, here, count_ref, take(12))
    cut = cut_of(width)
    sums = [
        SplitScatter(grid, here, parts[c], parts_sent[c], take(25), cut) for c in range(CHUNKS)
    ]
    spreads = [
        [
            Gather(grid, here, all_refs[c], take(6), (STAGES[1], STAGES[2]), slice(cut, width)),
            Gather(grid, here, all_refs[c], take(6), (STAGES[2], STAGES[1]), slice(0, cut)),
        ]
        for c in range(CHUNKS)
    ]
    own_rows = (slice(None),) + here[1:]
    sides = Scatter(grid, here, side_ref.at[own_rows], side_sent, take(5), STAGES[2:], ALL[:1])
    lefts = [
        Scatter(grid, here, left_ref.at[every + (cols,)], left_sent.at[every + (cols,)], take(15))
        for cols in halves
    ]

    def facts_copy(step):
        rows = pl.ds(pl.multiple_of(step * block, block), block)
        return pltpu.make_async_copy(facts_hbm.at[rows, :], facts_ref.at[rows, :], in_sems.at[step])

    others = [
        pltpu.make_async_copy(source, target, in_sems.at[4 + index])
        for index, (source, target) in enumerate([
            (owner_hbm, owner_ref), (slot_hbm, slot_ref), (w_hbm, w_ref),
            (w_upd_hbm, w_upd_ref), (cot_hbm, cot_ref), (feats_hbm, feats_ref),
        ])
    ]
    for copy in others[:3]:
        copy.start()
    for step in range(4):
        facts_copy(step).start()
    for copy in others[:2]:
        copy.wait()
    slot = slot_ref[...]
    pos_ref[...] = (
        lax.rem(slot, share) // piece * chunk
        + (owner_ref[...] * n_rep + slot // share) * piece
        + lax.rem(slot, piece)
    )

    def one_hot(rows, first, entries):
        ids = lax.broadcasted_iota(jnp.int32, (rows, fact_rows), 0) + first
        return (ids == entries).astype(f32).astype(bf16)

    def find_hits(first):
        return one_hot(rows_step, first, pos_ref[...])

    lines = count_ref.shape[0]
    table = lax.dot_general(
        one_hot(max(lines, 16), 0, pos_ref[...] // 128),
        one_hot(128, 0, lax.rem(pos_ref[...], 128)),
        (((1,), (1,)), ((), ())), preferred_element_type=f32,
    )
    count_ref[...] = table[0:lines]

    def hot_rows(first):
        if sum_steps == 1:
            return slice(first, first + rows_step)
        return pl.ds(pl.multiple_of(first, rows_step), rows_step)

    def prepare(step, carry):
        hot_ref[hot_rows(step * rows_step), :] = find_hits(step * rows_step)
        return carry

    if kept:
        repeat(sum_steps, prepare)
    others[2].wait()

    def project(first, count):
        for index in range(first, first + count):
            facts_copy(index).wait()
        rows = slice(first * block, (first + count) * block)
        half_pre = 0.5 * jnp.dot(facts_ref[rows, :], w_ref[...], preferred_element_type=f32)
        message_ref[rows, :] = (half_pre + half_pre * jnp.tanh(half_pre)).astype(bf16)

    for first, count in ((0, 2), (2, 2)):
        project(first, count)
    for copy in others[3:]:
        copy.start()

    for c in range(CHUNKS):

        def gather_sums(step, carry, c=c):
            first = c * chunk + step * rows_step
            hot = hot_ref[hot_rows(first), :] if kept else find_hits(first)
            agg = jnp.dot(hot, message_ref[...], preferred_element_type=f32)
            if kept and c + 1 < CHUNKS:
                hot_ref[hot_rows(first + chunk), :] = find_hits(first + chunk)
            agg = agg.reshape(tall, 2, grid[R_HI], 2, piece, width)
            parts[c][pl.ds(step * tall, tall)] = agg
            parts_sent[c][pl.ds(step * tall, tall)] = agg.astype(bf16)
            return carry

        repeat(sum_steps, gather_sums)
        if c == 0:
            pl.semaphore_wait(pltpu.get_barrier_semaphore(), greeted)
        sums[c].start()
        if c == 0:
            counts.start()

    def turn_facts(step, carry):
        rows = pl.ds(pl.multiple_of(step * block, block), block)
        facts_t[:, rows] = jnp.transpose(facts_ref[rows, :])
        return carry

    def open_gate(step, carry):
        rows = pl.ds(pl.multiple_of(step * 2 * block, 2 * block), 2 * block)
        pre = jnp.dot(facts_ref[rows, :], w_ref[...], preferred_element_type=f32)
        gate_ref[rows, :] = silu_grad(pre)
        return carry

    def hits_of(step, c):
        keys = jnp.concatenate([
            jnp.transpose(jnp.broadcast_to(
                pos_ref[:, pl.ds(pl.multiple_of(step * block + at, 128), 128)], (128, 128)
            ))
            for at in range(0, block, 128)
        ], axis=0)
        return jnp.concatenate([
            (keys == lax.broadcasted_iota(jnp.int32, (block, 128), 1) + (c * chunk + at))
            .astype(f32).astype(bf16)
            for at in range(0, chunk, 128)
        ], axis=1)

    def turn_hits(step, carry):
        rows = pl.ds(pl.multiple_of(step * block, block), block)
        for c in range(CHUNKS):
            hot_t[rows, c * chunk:(c + 1) * chunk] = hits_of(step, c)
        return carry

    def hits(step, c):
        if not kept:
            return hits_of(step, c)
        return hot_t[:, c * chunk:(c + 1) * chunk]

    def expand_rows(step):
        if expand_steps == 1:
            return slice(0, fact_rows)
        return pl.ds(pl.multiple_of(step * expand_block, expand_block), expand_block)

    sums[0].split()
    counts.advance()
    sums[1].split()
    for copy in others[3:]:
        copy.wait()
    w_upd_t[...] = jnp.transpose(w_upd_ref[...])
    w_t[...] = jnp.transpose(w_ref[...])
    lax.fori_loop(0, 4, turn_facts, 0)
    if kept:
        lax.fori_loop(0, 4, turn_hits, 0)
    sums[0].advance()
    counts.advance()
    sums[1].advance()
    lax.fori_loop(0, 2, open_gate, 0)

    def entity(c):
        first = c * chunk + (ent * n_rep + rep) * piece
        table = counts.table[...]
        line = jnp.sum(
            jnp.where(
                lax.broadcasted_iota(jnp.int32, table.shape, 0) == first // 128, table, 0.0
            ), axis=0, keepdims=True,
        )
        lane = lax.broadcasted_iota(jnp.int32, (piece, 128), 1)
        row = lax.broadcasted_iota(jnp.int32, (piece, 128), 0) + lax.rem(first, 128)
        count = jnp.sum(
            jnp.where(lane == row, jnp.broadcast_to(line, (piece, 128)), 0.0),
            axis=1, keepdims=True,
        )
        denom = jnp.maximum(count, 1.0)
        rows = slice(c * piece, (c + 1) * piece)
        mean = (sums[c].value() / denom).astype(bf16)
        zval = jnp.dot(mean, w_upd_ref[...], preferred_element_type=f32)
        grad_z = (cot_ref[rep, rows].astype(f32) * silu_grad(zval)).astype(bf16)
        d_mean = jnp.dot(grad_z, w_upd_t[...], preferred_element_type=f32)
        all_refs[c][here] = (d_mean / denom).astype(bf16)
        for item in spreads[c]:
            item.start()
        pair = pair_ref.at[here[1:] + (c,)]
        pair[:, 0:width] = mean
        pair[:, width:2 * width] = grad_z
        for place in group:
            index = len(pair_copies)
            pair_copies.append(
                send_to(place, pair, pair, pair_send.at[index], pair_recv.at[index])
            )

    group = peers_of(grid, here, STAGES[1])
    pair_copies = []
    counts.advance()
    for c in range(CHUNKS):
        sums[c].finish()
        entity(c)
    for item in spreads[0] + spreads[1]:
        item.second()
    for copy in pair_copies:
        copy.wait()
    pairs = pair_ref.at[:, :, here[R_LO]]
    other = peers_of(grid, here, STAGES[0])[0]
    pair_copy = send_to(other, pairs, pairs, core_send.at[0], core_recv.at[0])

    def expand_first(step, carry):
        spread_ref[expand_rows(step), :] = jnp.dot(
            hits(step, 0), all_refs[0][...].reshape(chunk, width), preferred_element_type=f32
        ).astype(bf16)
        return carry

    for item in spreads[0]:
        item.third()
    for item in spreads[0]:
        item.finish()
    repeat(expand_steps, expand_first)
    for item in spreads[1]:
        item.third()
    for item in spreads[1]:
        item.finish()

    for number, cols in enumerate(halves):

        def expand(step, carry, cols=cols):
            rows = expand_rows(step)
            table = all_refs[1][every + (cols,)].reshape(chunk, half)
            d_msg = spread_ref[rows, cols].astype(f32) + jnp.dot(
                hits(step, 1), table, preferred_element_type=f32
            )
            d_pre_ref[rows, cols] = (d_msg * gate_ref[rows, cols]).astype(bf16)
            return carry

        repeat(expand_steps, expand)
        left = jnp.dot(facts_t[...], d_pre_ref[:, cols], preferred_element_type=f32)
        left = left.reshape(left_ref.shape[:-1] + (half,))
        left_ref[every + (cols,)] = left
        left_sent[every + (cols,)] = left.astype(bf16)
        lefts[number].start()
    lefts[0].advance()
    pair_copy.wait()
    pair = pair_ref[...].reshape(2 * grid[R_HI] * 2 * share, 2 * width)
    side = lax.dot_general(
        pair[:, width:2 * width], pair[:, 0:width],
        (((0,), (0,)), ((), ())), preferred_element_type=f32,
    )
    side_ref[...] = side.reshape(side_ref.shape)
    side_sent[...] = side_ref[own_rows].astype(bf16)
    sides.start()
    lefts[1].advance()
    means = pair_ref[here[E_LO], :, :, :, :, 0:width].reshape(ent_rows, width)
    zval = jnp.dot(means, w_upd_ref[...], preferred_element_type=f32)
    feats = feats_ref[...].reshape(ent_rows, width).astype(f32)
    ent_out_ref[...] = (feats + zval * sigmoid(zval)).astype(bf16)

    grad_ref = facts_ref

    def grad_copy(step):
        rows = pl.ds(pl.multiple_of(step * block, block), block)
        return pltpu.make_async_copy(
            grad_ref.at[rows, :], fact_grad_hbm.at[rows, :], out_sems.at[step]
        )

    def fact_grads(step, carry):
        rows = pl.ds(pl.multiple_of(step * block, block), block)
        grad_ref[rows, :] = jnp.dot(
            d_pre_ref[rows, :], w_t[...], preferred_element_type=f32
        ).astype(bf16)
        grad_copy(step).start()
        return carry

    lax.fori_loop(0, 4, fact_grads, 0)
    for item in lefts:
        item.advance()
    sides.finish()
    side_out_ref[...] = sides.own[...]
    for step in range(4):
        grad_copy(step).wait()
    for item in lefts:
        item.advance()
    left_out_ref[:, 0:half] = lefts[0].own[...]
    left_out_ref[:, half:width] = lefts[1].own[...]


def write_kernel(*refs):
    count = (len(refs) - 1) // 2
    sources, targets, sems = refs[:count], refs[count:2 * count], refs[-1]
    copies = []
    for source, target in zip(sources, targets):
        pieces = 4 if source.shape[0] % 64 == 0 and source.shape[0] > 1024 else 1
        rows = source.shape[0] // pieces
        for piece in range(pieces):
            at = pl.ds(piece * rows, rows)
            copies.append(
                pltpu.make_async_copy(source.at[at], target.at[at], sems.at[len(copies)])
            )
    for copy in copies:
        copy.start()
    for copy in copies:
        copy.wait()


def in_vmem(number):
    return [pl.BlockSpec(memory_space=pltpu.VMEM)] * number


def anywhere(number):
    return [pl.BlockSpec(memory_space=pl.ANY)] * number


def in_hbm(number):
    return [pl.BlockSpec(memory_space=pltpu.HBM)] * number


def per_device(facts, fact_owner, fact_slot, entity_feats, out_cotangent, w_msg, w_upd):
    n_owners = lax.axis_size("ent")
    n_copies = lax.axis_size("rep")
    grid = (n_owners // 2, 2, n_copies // 2, 2)
    fact_rows, width = facts.shape
    ent_rows = entity_feats.shape[0]
    ents = ent_rows * n_owners
    share = ent_rows // n_copies
    piece = share // CHUNKS
    bf16, f32 = jnp.bfloat16, jnp.float32
    rows = width // (n_owners * n_copies)
    half = width // 2
    kept = ents <= 1024
    table = (ents // 128, 128)
    ent_out, fact_grad, left, side = pl.pallas_call(
        functools.partial(layer_kernel, grid, kept),
        out_shape=(
            jax.ShapeDtypeStruct((ent_rows, width), bf16),
            jax.ShapeDtypeStruct((fact_rows, width), bf16),
            jax.ShapeDtypeStruct((rows, width), f32),
            jax.ShapeDtypeStruct((rows, width), f32),
        ),
        in_specs=in_hbm(7),
        out_specs=in_vmem(1) + anywhere(1) + in_vmem(2),
        scratch_shapes=(
            [
                pltpu.VMEM((fact_rows, width), bf16),
                pltpu.VMEM((n_copies, share, width), bf16),
                pltpu.VMEM((n_copies, share, width), bf16),
                pltpu.VMEM((width, width), bf16),
                pltpu.VMEM((width, width), bf16),
                pltpu.SemaphoreType.DMA((10,)),
                pltpu.SemaphoreType.DMA((4,)),
                pltpu.VMEM((1, fact_rows), jnp.int32),
                pltpu.VMEM((1, fact_rows), jnp.int32),
                pltpu.VMEM((1, fact_rows), jnp.int32),
                pltpu.VMEM((fact_rows, width), f32),
                pltpu.VMEM((fact_rows, width), bf16),
                pltpu.VMEM((fact_rows, width), bf16),
                pltpu.VMEM((ents, fact_rows) if kept else (16, 128), bf16),
                pltpu.VMEM((fact_rows, ents) if kept else (16, 128), bf16),
                pltpu.VMEM((width, fact_rows), bf16),
                pltpu.VMEM((width, width), bf16),
                pltpu.VMEM((width, width), bf16),
            ]
            + [pltpu.VMEM(grid + (piece, width), f32)] * CHUNKS
            + [pltpu.VMEM(grid + (piece, width), bf16)] * (2 * CHUNKS)
            + [
                pltpu.VMEM(table, f32),
                pltpu.VMEM(grid[1:] + (CHUNKS, piece, 2 * width), bf16),
                pltpu.SemaphoreType.DMA((CHUNKS * peer_count(grid, STAGES[1]),)),
                pltpu.SemaphoreType.DMA((CHUNKS * peer_count(grid, STAGES[1]),)),
                pltpu.SemaphoreType.DMA((1,)),
                pltpu.SemaphoreType.DMA((1,)),
            ]
            + [
                pltpu.VMEM(grid + (rows, width), f32),
                pltpu.VMEM((grid[E_HI], rows, width), bf16),
                pltpu.VMEM(grid + (rows, width), f32),
                pltpu.VMEM(grid + (rows, width), bf16),
            ]
            + count_scratch(grid, table)
            + split_scratch(grid, piece, width, cut_of(width), bf16) * CHUNKS
            + (gather_scratch(grid, (STAGES[1], STAGES[2]))
               + gather_scratch(grid, (STAGES[2], STAGES[1]))) * CHUNKS
            + sum_scratch(grid, (rows, width), bf16, STAGES[2:], ALL[:1])
            + sum_scratch(grid, (rows, half), bf16) * 2
        ),
        compiler_params=pltpu.CompilerParams(
            collective_id=0, has_side_effects=True, vmem_limit_bytes=(48 if kept else 60) << 20
        ),
    )(*[
        pltpu.with_memory_space_constraint(operand, pltpu.HBM)
        for operand in (
            facts,
            fact_owner.reshape(1, fact_rows),
            fact_slot.reshape(1, fact_rows),
            entity_feats.reshape(n_copies, share, width),
            out_cotangent.reshape(n_copies, share, width),
            w_msg,
            w_upd,
        )
    ])
    results = (ent_out, fact_grad, left, side)
    return pl.pallas_call(
        write_kernel,
        out_shape=tuple(jax.ShapeDtypeStruct(r.shape, r.dtype) for r in results),
        in_specs=anywhere(4),
        out_specs=in_hbm(4),
        scratch_shapes=[pltpu.SemaphoreType.DMA((8,))],
        compiler_params=pltpu.CompilerParams(vmem_limit_bytes=4 << 20),
    )(*results)


def solution(mesh):
    placed = (
        P(("ent", "rep"), None),
        P(("ent", "rep"), None),
        P(("ent", "rep")),
        P("ent", None),
        P("ent", None),
        P(),
        P(),
    )
    return jax.shard_map(
        per_device,
        mesh=mesh,
        in_specs=placed,
        out_specs=(
            P("ent", None),
            P(("ent", "rep"), None),
            P(("ent", "rep"), None),
            P(("ent", "rep"), None),
        ),
        check_vma=False,
    )
```
